32 devices in a mesh: dp: 4 (over z), cent: 8 (over y, x, core).
Axes of the slice: x: 2, y: 2, z: 4, core: 2. Of those that a mesh axis runs over, the one named last changes fastest.
Arguments:
- vectors: bfloat16 [8192, 768], P('dp'), may hold values from -30 to 30
- centroids: bfloat16 [16384, 768], P('cent'), may hold values from -1 to 1
- assignment: int32 [8192], P(('dp', 'cent')), may hold values from 0 to 16383, as said below
Outputs:
- new_centroids: bfloat16 [16384, 768], P('cent')
- row_potential: float32 [8192], P('dp')
- column_potential: float32 [16384], P('cent')
- residuals: bfloat16 [8192, 768], P(('dp', 'cent'))
The draws below stay inside these ranges and needn't reach their ends.
Inputs may be any that keep to these rules, and one draw needn't show every extreme that they name: `assignment`: the entry's centroid is owned by index entry // 2048 of cent. In each aligned block of 256 entries (the rows of one device), at most 64 entries name centroids of one owning index; one owning index, drawn from the seed, receives exactly 64 entries from every block.
All inputs are finite; a program needn't handle non-finite values.
Results may differ from the reference program's by a relative error of at most 0.00705.
Values may be sent and summed in bfloat16 or wider, within the bound.
No kernel may reach another device: no remote copies, remote signals or barrier semaphores. Data moves between devices by JAX's collectives and lax.ppermute only.
A program may use at most 128 MiB of HBM per device.

```python
import math
import jax
import jax.numpy as jnp

D = 768
K_DEV = 2048
ITERS = 3
SLAB = 8192
LISTS = 16384
SEND_ROWS = 256
CAP = 64
N_CENT = 8


def shared_floats(key):
    base = jax.random.fold_in(key, 7)
    vector_key, centre_key = jax.random.split(base, 2)
    centres = jax.random.normal(centre_key, (LISTS, D), jnp.float32) / math.sqrt(D)
    points = jax.random.normal(vector_key, (SLAB, D), jnp.float32)
    return (jnp.clip(points, -30.0, 30.0), jnp.clip(centres, -1.0, 1.0))


def draw_vectors(key, part):
    points, centres = shared_floats(key)
    return points.astype(jnp.bfloat16)


def draw_centroids(key, part):
    points, centres = shared_floats(key)
    return centres.astype(jnp.bfloat16)


def draw_assignment(key, part):
    blocks = SLAB // SEND_ROWS
    first_key, order_key, local_key = jax.random.split(jax.random.fold_in(key, 11), 3)
    favored = jax.random.randint(first_key, (), 0, N_CENT).astype(jnp.int32)
    others = (jnp.arange((N_CENT - 1) * CAP) // CAP).astype(jnp.int32)
    others = others + (others >= favored).astype(jnp.int32)

    def one_block(block_key):
        choose_key, mixing_key = jax.random.split(block_key)
        chosen = jax.random.permutation(choose_key, others)[:SEND_ROWS - CAP]
        targets = jnp.concatenate([jnp.full((CAP,), favored, jnp.int32), chosen.astype(jnp.int32)])
        return jax.random.permutation(mixing_key, targets)
    targets = jax.vmap(one_block)(jax.random.split(order_key, blocks))
    local_ids = jax.random.randint(local_key, (blocks, SEND_ROWS), 0, K_DEV).astype(jnp.int32)
    return (targets * K_DEV + local_ids).reshape(SLAB).astype(jnp.int32)


def setup_inputs(seed: int = 0) -> dict:
    key_of = jax.random.split(jax.random.key(seed), 4)
    vectors = draw_vectors(jax.random.fold_in(key_of[3], 71), 0)
    centroids = draw_centroids(jax.random.fold_in(key_of[3], 71), 0)
    assignment = draw_assignment(jax.random.fold_in(key_of[3], 71), 0)
    return {"vectors": vectors, "centroids": centroids, "assignment": assignment}


inv_temp = 2.0


def log_total(values, axis):
    highest = jnp.max(values, axis=axis, keepdims=True)
    return jnp.squeeze(highest, axis) + jnp.log(jnp.sum(jnp.exp(values - highest), axis=axis))


def reference(vectors, centroids, assignment):
    logits = inv_temp * jnp.dot(vectors, centroids.T, preferred_element_type=jnp.float32)
    log_mass = math.log(SLAB / LISTS)
    row_potential = jnp.zeros((SLAB,), jnp.float32)
    column_potential = jnp.zeros((LISTS,), jnp.float32)
    for iteration in range(ITERS):
        column_potential = log_mass - log_total(logits + row_potential[:, None], 0)
        row_potential = -log_total(logits + column_potential[None, :], 1)
    plan = jnp.exp(logits + row_potential[:, None] + column_potential[None, :]).astype(jnp.bfloat16)
    numerator = jnp.dot(plan.T, vectors, preferred_element_type=jnp.float32)
    mass = jnp.sum(plan.astype(jnp.float32), axis=0)
    new_centroids = (numerator / mass[:, None]).astype(jnp.bfloat16)
    chosen = new_centroids[assignment.astype(jnp.int32)]
    residuals = (vectors.astype(jnp.float32) - chosen.astype(jnp.float32)).astype(jnp.bfloat16)
    return (new_centroids, row_potential, column_potential, residuals)
```

```python
import functools
import math

import jax
import jax.numpy as jnp
from jax import lax
from jax.experimental import pallas as pl
from jax.experimental.pallas import tpu as pltpu
from jax.sharding import PartitionSpec as P

ITERS = 3


F32 = jnp.float32
BF16 = jnp.bfloat16
NT = (((1,), (1,)), ((), ()))
NN = (((1,), (0,)), ((), ()))


def cost(flops, moved, exps=0):
    return pl.CostEstimate(flops=int(flops), bytes_accessed=int(moved), transcendentals=int(exps))


def logits_kernel(v_ref, c_ref, l_ref, stat_ref, *, chunk):
    doubled = c_ref[...] * 2
    rows = v_ref.shape[0]
    peak, total = None, None
    for start in range(0, rows, chunk):
        part = lax.dot_general(
            v_ref[start : start + chunk, :], doubled, NT, preferred_element_type=F32
        )
        l_ref[start : start + chunk, :] = part
        part_peak = jnp.max(part, axis=0, keepdims=True)
        higher = part_peak if peak is None else jnp.maximum(peak, part_peak)
        part_total = jnp.sum(jnp.exp(part - higher), axis=0, keepdims=True)
        total = part_total if peak is None else total * jnp.exp(peak - higher) + part_total
        peak = higher
    stat_ref[0:1, :] = peak
    stat_ref[1:2, :] = total


def logits_and_stats(vectors, centroids):
    rows, width = vectors.shape
    lists = centroids.shape[0]
    tile = min(512, lists)
    return pl.pallas_call(
        functools.partial(logits_kernel, chunk=min(512, rows)),
        grid=(lists // tile,),
        in_specs=[
            pl.BlockSpec((rows, width), lambda j: (0, 0)),
            pl.BlockSpec((tile, width), lambda j: (j, 0)),
        ],
        out_specs=[
            pl.BlockSpec((rows, tile), lambda j: (0, j)),
            pl.BlockSpec((2, tile), lambda j: (0, j)),
        ],
        out_shape=[
            jax.ShapeDtypeStruct((rows, lists), F32),
            jax.ShapeDtypeStruct((2, lists), F32),
        ],
        cost_estimate=cost(2 * rows * lists * width, 4 * rows * lists, rows * lists),
        name="logits_stats",
    )(vectors, centroids)


def first_rows_kernel(l_ref, c_ref, m_ref, stat_ref):
    shifted = l_ref[...] + c_ref[...]
    peak = jnp.max(shifted, axis=1, keepdims=True)
    scaled = jnp.exp(shifted - peak)
    m_ref[...] = scaled.astype(BF16)
    total = jnp.sum(scaled, axis=1, keepdims=True)
    rows = shifted.shape[0]
    stat_ref[0:1, :] = jnp.transpose(jnp.broadcast_to(peak, (rows, 128)))[0:1, :]
    stat_ref[1:2, :] = jnp.transpose(jnp.broadcast_to(total, (rows, 128)))[0:1, :]


def first_rows(logits, column):
    rows, lists = logits.shape
    tile = min(256, rows)
    return pl.pallas_call(
        first_rows_kernel,
        grid=(rows // tile,),
        in_specs=[
            pl.BlockSpec((tile, lists), lambda i: (i, 0)),
            pl.BlockSpec((1, lists), lambda i: (0, 0)),
        ],
        out_specs=[
            pl.BlockSpec((tile, lists), lambda i: (i, 0)),
            pl.BlockSpec((2, tile), lambda i: (0, i)),
        ],
        out_shape=[
            jax.ShapeDtypeStruct((rows, lists), BF16),
            jax.ShapeDtypeStruct((2, rows), F32),
        ],
        cost_estimate=cost(4 * rows * lists, 6 * rows * lists, rows * lists),
        name="first_rows",
    )(logits, column)


def three_parts(value):
    head = value.astype(BF16)
    rest = value - head.astype(F32)
    middle = rest.astype(BF16)
    last = (rest - middle.astype(F32)).astype(BF16)
    zero = jnp.zeros((5, value.shape[1]), BF16)
    return jnp.concatenate([head, middle, last, zero], axis=0)


def column_sum_kernel(a_ref, m_ref, out_ref):
    sums = lax.dot_general(three_parts(a_ref[...]), m_ref[...], NN, preferred_element_type=F32)
    out_ref[...] = (sums[2:3] + sums[1:2]) + sums[0:1]


def column_sums(weights, scaled):
    rows, lists = scaled.shape
    tile = min(512, lists)
    return pl.pallas_call(
        column_sum_kernel,
        grid=(lists // tile,),
        in_specs=[
            pl.BlockSpec((1, rows), lambda j: (0, 0)),
            pl.BlockSpec((rows, tile), lambda j: (0, j)),
        ],
        out_specs=pl.BlockSpec((1, tile), lambda j: (0, j)),
        out_shape=jax.ShapeDtypeStruct((1, lists), F32),
        cost_estimate=cost(16 * rows * lists, 2 * rows * lists),
        name="column_sums",
    )(weights, scaled)


def row_sum_kernel(b_ref, m_ref, out_ref):
    sums = lax.dot_general(three_parts(b_ref[...]), m_ref[...], NT, preferred_element_type=F32)
    out_ref[...] = (sums[2:3] + sums[1:2]) + sums[0:1]


def row_sums(weights, scaled):
    rows, lists = scaled.shape
    tile = min(512, rows)
    return pl.pallas_call(
        row_sum_kernel,
        grid=(rows // tile,),
        in_specs=[
            pl.BlockSpec((1, lists), lambda i: (0, 0)),
            pl.BlockSpec((tile, lists), lambda i: (i, 0)),
        ],
        out_specs=pl.BlockSpec((1, tile), lambda i: (0, i)),
        out_shape=jax.ShapeDtypeStruct((1, rows), F32),
        cost_estimate=cost(16 * rows * lists, 2 * rows * lists),
        name="row_sums",
    )(weights, scaled)


def plan_kernel(*refs, earlier, final, row_steps):
    c_ref, col_ref, v_ref, r_ref = refs[:4]
    before = refs[4 : 4 + 2 * earlier]
    outs = refs[4 + 2 * earlier : -3]
    acc, mass, col = refs[-3:]
    step = pl.program_id(1)
    tile = c_ref.shape[0]

    @pl.when(step == 0)
    def _():
        acc[...] = jnp.zeros_like(acc)
        mass[...] = jnp.zeros_like(mass)
        col[...] = jnp.transpose(jnp.broadcast_to(col_ref[...], (128, tile)))

    rows = v_ref.shape[0]
    half = min(256, tile)
    for start in range(0, tile, half):
        part = slice(start, start + half)
        logits = lax.dot_general(
            c_ref[part, :] * 2, v_ref[...], NT, preferred_element_type=F32
        )
        plan = jnp.exp(logits + r_ref[...] + col[part, 0:1]).astype(BF16)
        acc[part, :] += lax.dot_general(plan, v_ref[...], NN, preferred_element_type=F32)
        wide = plan.astype(F32)
        sums = wide[:, 0:128]
        for lane in range(128, rows, 128):
            sums = sums + wide[:, lane : lane + 128]
        mass[part, :] += sums

    @pl.when(step == row_steps - 1)
    def _():
        numerator, weight = acc[...], mass[...]
        if earlier == 2:
            numerator = before[2][...] + numerator
            weight = before[3][...] + weight
        if earlier:
            numerator = before[0][...] + numerator
            weight = before[1][...] + weight
        if final:
            outs[0][...] = (numerator / jnp.sum(weight, axis=1, keepdims=True)).astype(BF16)
        else:
            outs[0][...] = numerator
            outs[1][...] = weight


def plan_sums(centroids, column, vectors, row, before=(), final=False):
    rows, width = vectors.shape
    lists = centroids.shape[0]
    tile, depth = min(512, lists), min(1024, rows)
    steps = rows // depth
    sums = pl.BlockSpec((tile, width), lambda j, i: (j, 0))
    masses = pl.BlockSpec((tile, 128), lambda j, i: (j, 0))
    flat = [item for pair in before for item in pair]
    if final:
        out_specs, out_shape = sums, jax.ShapeDtypeStruct((lists, width), BF16)
    else:
        out_specs = [sums, masses]
        out_shape = [
            jax.ShapeDtypeStruct((lists, width), F32),
            jax.ShapeDtypeStruct((lists, 128), F32),
        ]
    return pl.pallas_call(
        functools.partial(plan_kernel, earlier=len(before), final=final, row_steps=steps),
        grid=(lists // tile, steps),
        in_specs=[
            pl.BlockSpec((tile, width), lambda j, i: (j, 0)),
            pl.BlockSpec((1, tile), lambda j, i: (0, j)),
            pl.BlockSpec((depth, width), lambda j, i: (i, 0)),
            pl.BlockSpec((1, depth), lambda j, i: (0, i)),
        ]
        + [sums, masses] * len(before),
        out_specs=out_specs,
        out_shape=out_shape,
        scratch_shapes=[
            pltpu.VMEM((tile, width), F32),
            pltpu.VMEM((tile, 128), F32),
            pltpu.VMEM((tile, 128), F32),
        ],
        cost_estimate=cost(4 * rows * lists * width, 4 * lists * width, rows * lists),
        name="plan_sums",
    )(centroids, column, vectors, row, *flat)


def swap(value, axis, key):
    count = lax.axis_size(axis)
    return lax.ppermute(value, axis, [(i, i ^ key) for i in range(count)])


def tree(parts, join):
    while len(parts) > 1:
        parts = [join(parts[k], parts[k + 1]) for k in range(0, len(parts), 2)]
    return parts[0]


def everywhere(value, axis):
    return [value] + [swap(value, axis, key) for key in range(1, lax.axis_size(axis))]


def spread(value, axis):
    count = lax.axis_size(axis)
    return lax.all_to_all(
        jnp.broadcast_to(value[None], (count,) + value.shape), axis, 0, 0, tiled=True
    )


def after(value, *others):
    return lax.optimization_barrier((value,) + others)[0]


def on_device(vectors, centroids, assignment):
    row_count, width = vectors.shape
    list_count = centroids.shape[0]
    data_count = lax.axis_size("dp")
    owner_count = lax.axis_size("cent")
    me = lax.axis_index("cent")
    send_count = row_count // owner_count
    capacity = max(2, 2 * send_count // owner_count)
    ratio = row_count * data_count / (list_count * owner_count)
    log_mass = math.log(ratio)

    slices = vectors.reshape(owner_count, send_count, width)
    own = lax.dynamic_index_in_dim(slices, me, 0, keepdims=False)
    keys = list(range(0, owner_count, 2)) + list(range(1, owner_count, 2))
    order = jnp.bitwise_xor(me, jnp.array(keys, jnp.int32))

    def arranged(row):
        return row.reshape(owner_count, send_count)[order].reshape(1, row_count)

    targets = assignment // list_count
    local_ids = assignment % list_count
    positions = jnp.arange(send_count, dtype=jnp.int32)
    earlier_same = (targets[:, None] == targets[None, :]) & (
        positions[None, :] < positions[:, None]
    )
    ranks = jnp.sum(earlier_same.astype(jnp.int32), axis=1)
    slots = targets * capacity + ranks
    picked = slots[:, None] == jnp.arange(owner_count * capacity, dtype=jnp.int32)[None, :]
    outgoing_ids = jnp.sum(jnp.where(picked, local_ids[:, None], 0), axis=0)
    arrived_ids = lax.all_to_all(
        outgoing_ids.reshape(owner_count, capacity), "cent", 0, 0, tiled=True
    )

    logits, stats = logits_and_stats(vectors, centroids)
    stats = everywhere(stats, "dp")
    peak = tree([s[0:1] for s in stats], jnp.maximum)
    total = tree([s[1:2] * jnp.exp(s[0:1] - peak) for s in stats], jnp.add)
    first_column = log_mass - (peak + jnp.log(total))

    scaled, stats = first_rows(logits, first_column)
    local_peak = stats[0:1]
    stats = spread(stats, "cent")
    row_peak = jnp.max(stats[:, 0, :], axis=0)[None]
    total = jnp.sum(stats[:, 1, :] * jnp.exp(stats[:, 0, :] - row_peak), axis=0)[None]
    row = -(row_peak + jnp.log(total))
    share = jnp.exp(local_peak - row_peak)
    column = first_column
    for _ in range(ITERS - 1):
        sums = column_sums(jnp.exp(local_peak + row), scaled)
        total = tree(everywhere(sums, "dp"), jnp.add)
        column = first_column + (log_mass - jnp.log(total))
        sums = row_sums(ratio / total, scaled) * share
        total = jnp.sum(spread(sums, "cent"), axis=0)
        row = -(row_peak + jnp.log(total))

    blocks = [slices[order].reshape(row_count, width)]
    block_rows = [arranged(row)]
    for key in range(1, data_count):
        piece = swap(own if key == 1 else after(own, column), "dp", key)
        piece = after(piece, row)
        pieces = [piece] + [swap(piece, "cent", step) for step in range(2, owner_count, 2)]
        half = jnp.concatenate(pieces, axis=0)
        other = swap(half, "cent", 1)
        blocks.append(jnp.concatenate([half, other], axis=0))
        block_rows.append(arranged(swap(row, "dp", key)))

    pair = ()
    held = ()
    for index in range(data_count):
        last = index == data_count - 1
        if index % 2 == 0:
            pair = plan_sums(centroids, column, blocks[index], block_rows[index])
        else:
            before = held + (pair,)
            result = plan_sums(
                centroids, column, blocks[index], block_rows[index], before, final=last
            )
            held = (result,)
    updated = held[0]

    wanted = arrived_ids.reshape(-1)[:, None] == jnp.arange(list_count, dtype=jnp.int32)[None, :]
    rows = jnp.dot(wanted.astype(BF16), updated, preferred_element_type=BF16)
    returned = lax.all_to_all(
        rows.reshape(owner_count, capacity, width), "cent", 0, 0, tiled=True
    ).reshape(owner_count * capacity, width)
    chosen = jnp.dot(picked.astype(BF16), returned, preferred_element_type=F32)
    residuals = (own.astype(F32) - chosen).astype(BF16)
    return (updated, row.reshape(row_count), column.reshape(list_count), residuals)


def solution(mesh):
    in_specs = (P("dp", None), P("cent", None), P(("dp", "cent")))
    out_specs = (P("cent", None), P("dp"), P("cent"), P(("dp", "cent"), None))
    return jax.shard_map(
        on_device, mesh=mesh, in_specs=in_specs, out_specs=out_specs, check_vma=False
    )
```

```python
import functools
import math

import jax
import jax.numpy as jnp
from jax import lax
from jax.experimental import pallas as pl
from jax.experimental.pallas import tpu as pltpu
from jax.sharding import PartitionSpec as P

ITERS = 3


F32 = jnp.float32
BF16 = jnp.bfloat16
NT = (((1,), (1,)), ((), ()))
NN = (((1,), (0,)), ((), ()))
MIB = 1 << 20


def cost(flops, moved, exps=0):
    return pl.CostEstimate(flops=int(flops), bytes_accessed=int(moved), transcendentals=int(exps))


def grant(mib):
    return pltpu.CompilerParams(vmem_limit_bytes=mib * MIB)


def tree(parts, join):
    while len(parts) > 1:
        parts = [join(parts[k], parts[k + 1]) for k in range(0, len(parts), 2)]
    return parts[0]


def join_pairs(parts):
    peak = tree([part[0:1] for part in parts], jnp.maximum)
    total = tree([part[1:2] * jnp.exp(part[0:1] - peak) for part in parts], jnp.add)
    return peak, total


def whole(shape):
    return pl.BlockSpec(shape, lambda *_: (0,) * len(shape))


def logits_kernel(v_ref, c_ref, l_ref, stat_ref, *, chunk):
    doubled = c_ref[...] * 2
    rows = v_ref.shape[0]
    peak, total = None, None
    for start in range(0, rows, chunk):
        part = lax.dot_general(
            v_ref[start : start + chunk, :], doubled, NT, preferred_element_type=F32
        )
        l_ref[start : start + chunk, :] = part
        part_peak = jnp.max(part, axis=0, keepdims=True)
        higher = part_peak if peak is None else jnp.maximum(peak, part_peak)
        part_total = jnp.sum(jnp.exp(part - higher), axis=0, keepdims=True)
        total = part_total if peak is None else total * jnp.exp(peak - higher) + part_total
        peak = higher
    stat_ref[0:1, :] = peak
    stat_ref[1:2, :] = total


def logits_and_stats(vectors, centroids):
    rows, width = vectors.shape
    lists = centroids.shape[0]
    tile = min(256, lists)
    return pl.pallas_call(
        functools.partial(logits_kernel, chunk=min(1024, rows)),
        grid=(lists // tile,),
        in_specs=[whole((rows, width)), pl.BlockSpec((tile, width), lambda j: (j, 0))],
        out_specs=[
            pl.BlockSpec((rows, tile), lambda j: (0, j)),
            pl.BlockSpec((2, tile), lambda j: (0, j)),
        ],
        out_shape=[
            jax.ShapeDtypeStruct((rows, lists), F32),
            jax.ShapeDtypeStruct((2, lists), F32),
        ],
        compiler_params=grant(24),
        cost_estimate=cost(2 * rows * lists * width, 4 * rows * lists, rows * lists),
        name="logits_stats",
    )(vectors, centroids)


def first_rows_kernel(*refs, parts, log_mass, group):
    l_ref, ids_ref = refs[0:2]
    stats = refs[2 : 2 + parts]
    m_ref, stat_ref, col_ref, peaks, totals = refs[2 + parts :]

    @pl.when(pl.program_id(0) == 0)
    def _():
        peak, total = join_pairs([part[...] for part in stats])
        col_ref[...] = log_mass - (peak + jnp.log(total))

    tile = l_ref.shape[0]

    def some(step, carry):
        rows = pl.ds(pl.multiple_of(step * group, group), group)
        shifted = l_ref[rows, :] + col_ref[...]
        peak = jnp.max(shifted, axis=1, keepdims=True)
        scaled = jnp.exp(shifted - peak)
        m_ref[rows, :] = scaled.astype(BF16)
        peaks[rows, :] = jnp.broadcast_to(peak, (group, 128))
        totals[rows, :] = jnp.broadcast_to(jnp.sum(scaled, axis=1, keepdims=True), (group, 128))
        return carry

    lax.fori_loop(0, tile // group, some, 0, unroll=4)
    stat_ref[0:1, :] = jnp.transpose(peaks[...])[0:1, :]
    stat_ref[1:2, :] = jnp.transpose(totals[...])[0:1, :]
    stat_ref[2:3, :] = ids_ref[...]


def first_rows(logits, ids, stats, log_mass):
    rows, lists = logits.shape
    tile = min(256, rows)
    return pl.pallas_call(
        functools.partial(first_rows_kernel, parts=len(stats), log_mass=log_mass, group=16),
        grid=(rows // tile,),
        in_specs=[
            pl.BlockSpec((tile, lists), lambda i: (i, 0)),
            pl.BlockSpec((1, tile), lambda i: (0, i)),
        ]
        + [whole((2, lists))] * len(stats),
        out_specs=[
            pl.BlockSpec((tile, lists), lambda i: (i, 0)),
            pl.BlockSpec((3, tile), lambda i: (0, i)),
            whole((1, lists)),
        ],
        out_shape=[
            jax.ShapeDtypeStruct((rows, lists), BF16),
            jax.ShapeDtypeStruct((3, rows), F32),
            jax.ShapeDtypeStruct((1, lists), F32),
        ],
        scratch_shapes=[pltpu.VMEM((tile, 128), F32), pltpu.VMEM((tile, 128), F32)],
        compiler_params=grant(16),
        cost_estimate=cost(4 * rows * lists, 6 * rows * lists, rows * lists),
        name="first_rows",
    )(logits, ids, *stats)


def store_parts(where, value):
    head = value.astype(BF16)
    rest = value - head.astype(F32)
    middle = rest.astype(BF16)
    last = (rest - middle.astype(F32)).astype(BF16)
    zero = jnp.zeros((5, value.shape[1]), BF16)
    where[...] = jnp.concatenate([head, middle, last, zero], axis=0)


def add_parts(sums):
    return (sums[2:3] + sums[1:2]) + sums[0:1]


def column_sum_kernel(*refs, parts, first):
    m_ref, own_ref = refs[0:2]
    stats = refs[2 : 2 + parts]
    if first:
        out_ref, peak_ref, weights = refs[2 + parts :]
    else:
        peak_ref = refs[2 + parts]
        out_ref, weights = refs[3 + parts :]

    @pl.when(pl.program_id(0) == 0)
    def _():
        if first:
            peak, total = join_pairs([part[...] for part in stats])
            peak_ref[...] = peak
        else:
            peak = peak_ref[...]
            total = tree([part[...] for part in stats], jnp.add)
        store_parts(weights, jnp.exp(own_ref[0:1, :] - (peak + jnp.log(total))))

    out_ref[...] = add_parts(
        lax.dot_general(weights[...], m_ref[...], NN, preferred_element_type=F32)
    )


def column_sums(scaled, own, stats, peak=None):
    rows, lists = scaled.shape
    tile = min(512, lists)
    first = peak is None
    row = whole((1, rows))
    out_specs = [pl.BlockSpec((1, tile), lambda j: (0, j))]
    out_shape = [jax.ShapeDtypeStruct((1, lists), F32)]
    return pl.pallas_call(
        functools.partial(column_sum_kernel, parts=len(stats), first=first),
        grid=(lists // tile,),
        in_specs=[pl.BlockSpec((rows, tile), lambda j: (0, j)), whole(own.shape)]
        + [whole(stats[0].shape)] * len(stats)
        + ([] if first else [row]),
        out_specs=out_specs + ([row] if first else []),
        out_shape=out_shape + ([jax.ShapeDtypeStruct((1, rows), F32)] if first else []),
        scratch_shapes=[pltpu.VMEM((8, rows), BF16)],
        compiler_params=grant(16),
        cost_estimate=cost(16 * rows * lists, 2 * rows * lists),
        name="column_sums",
    )(scaled, own, *stats, *([] if first else [peak]))


def row_sum_kernel(*refs, parts, ratio, log_mass):
    m_ref, first_ref, own_ref, peak_ref = refs[0:4]
    stats = refs[4 : 4 + parts]
    out_ref, col_ref, weights = refs[4 + parts :]

    @pl.when(pl.program_id(0) == 0)
    def _():
        total = tree([part[...] for part in stats], jnp.add)
        store_parts(weights, ratio / total)
        col_ref[...] = first_ref[...] + (log_mass - jnp.log(total))

    sums = add_parts(lax.dot_general(weights[...], m_ref[...], NT, preferred_element_type=F32))
    out_ref[...] = sums * jnp.exp(own_ref[0:1, :] - peak_ref[...])


def row_sums(scaled, first_column, own, peak, stats, ratio):
    rows, lists = scaled.shape
    tile = min(512, rows)
    column = whole((1, lists))
    return pl.pallas_call(
        functools.partial(
            row_sum_kernel, parts=len(stats), ratio=ratio, log_mass=math.log(ratio)
        ),
        grid=(rows // tile,),
        in_specs=[
            pl.BlockSpec((tile, lists), lambda i: (i, 0)),
            column,
            pl.BlockSpec((own.shape[0], tile), lambda i: (0, i)),
            pl.BlockSpec((1, tile), lambda i: (0, i)),
        ]
        + [column] * len(stats),
        out_specs=[pl.BlockSpec((1, tile), lambda i: (0, i)), column],
        out_shape=[
            jax.ShapeDtypeStruct((1, rows), F32),
            jax.ShapeDtypeStruct((1, lists), F32),
        ],
        scratch_shapes=[pltpu.VMEM((8, lists), BF16)],
        compiler_params=grant(16),
        cost_estimate=cost(16 * rows * lists, 2 * rows * lists),
        name="row_sums",
    )(scaled, first_column, own, peak, *stats)


def plan_kernel(*refs, planes, owners, depth):
    place_ref, c_ref, col_ref = refs[0:3]
    rows_in = refs[3 : 3 + planes]
    own_ref = refs[3 + planes]
    halves = refs[4 + planes : 4 + planes + 2 * (planes - 1)]
    out_ref, held, row_all, acc, mass, sems = refs[4 + planes + 2 * (planes - 1) :]
    tile = c_ref.shape[0]
    count = own_ref.shape[0]
    piece = count // owners
    plane, owner = place_ref[0], place_ref[1]

    def block(index):
        return pl.ds(pl.multiple_of(index * count, count), count)

    @pl.when(pl.program_id(0) == 0)
    def _():
        pltpu.make_async_copy(own_ref, held.at[block(plane)], sems.at[0]).start()
        row_all[pl.ds(plane, 1), :] = rows_in[0][...]
        for key in range(1, planes):
            other = plane ^ key
            row_all[pl.ds(other, 1), :] = rows_in[key][...]
            for index in range(owners):
                source = halves[2 * (key - 1) + index // (owners // 2)]
                at = (index % (owners // 2)) * piece
                slot = 2 * (index % (owners // 2)) + index // (owners // 2)
                start = pl.multiple_of(other * count + (owner ^ slot) * piece, piece)
                pltpu.make_async_copy(
                    source.at[pl.ds(at, piece)], held.at[pl.ds(start, piece)], sems.at[key]
                ).start()

    doubled = c_ref[...] * 2
    column = jnp.transpose(jnp.broadcast_to(col_ref[...], (128, tile)))[:, 0:1]
    steps = planes * count // depth

    def logits(step):
        here = held[step * depth : (step + 1) * depth, :]
        return lax.dot_general(doubled, here, NT, preferred_element_type=F32)

    @pl.when(pl.program_id(0) == 0)
    def _():
        for key in range(planes):
            pltpu.make_async_copy(held.at[block(key)], held.at[block(key)], sems.at[key]).wait()

    ready = logits(0)
    for step in range(steps):
        following = logits(step + 1) if step + 1 < steps else None
        start = step * depth
        row = row_all[start // count : start // count + 1, start % count : start % count + depth]
        plan = jnp.exp(ready + row + column).astype(BF16)
        part = lax.dot_general(
            plan, held[start : start + depth, :], NN, preferred_element_type=F32
        )
        wide = plan.astype(F32)
        sums = wide[:, 0:128]
        for lane in range(128, depth, 128):
            sums = sums + wide[:, lane : lane + 128]
        acc[...] = part if step == 0 else acc[...] + part
        mass[...] = sums if step == 0 else mass[...] + sums
        ready = following
    out_ref[...] = (acc[...] / jnp.sum(mass[...], axis=1, keepdims=True)).astype(BF16)


def new_centroids(place, centroids, column, rows, own, halves, owners):
    count, width = own.shape
    lists = centroids.shape[0]
    planes = len(rows)
    tile, depth = min(256, lists), min(1024, count)
    anywhere = pl.BlockSpec(memory_space=pl.ANY)
    total = planes * count
    return pl.pallas_call(
        functools.partial(plan_kernel, planes=planes, owners=owners, depth=depth),
        grid=(lists // tile,),
        in_specs=[
            pl.BlockSpec(memory_space=pltpu.SMEM),
            pl.BlockSpec((tile, width), lambda j: (j, 0)),
            pl.BlockSpec((1, tile), lambda j: (0, j)),
        ]
        + [whole((1, count))] * planes
        + [anywhere] * (1 + len(halves)),
        out_specs=pl.BlockSpec((tile, width), lambda j: (j, 0)),
        out_shape=jax.ShapeDtypeStruct((lists, width), BF16),
        scratch_shapes=[
            pltpu.VMEM((total, width), BF16),
            pltpu.VMEM((max(8, planes), count), F32),
            pltpu.VMEM((tile, width), F32),
            pltpu.VMEM((tile, 128), F32),
            pltpu.SemaphoreType.DMA((planes,)),
        ],
        compiler_params=grant(40),
        cost_estimate=cost(4 * total * lists * width, 2 * total * width, total * lists),
        name="new_centroids",
    )(place, centroids, column, *rows, own, *halves)


def pick_kernel(ids_ref, table_ref, *outs):
    count, lists = ids_ref.shape[0], table_ref.shape[0]
    wanted = ids_ref[...] == lax.broadcasted_iota(jnp.int32, (count, lists), 1)
    rows = lax.dot_general(
        wanted.astype(F32).astype(BF16), table_ref[...], NN, preferred_element_type=F32
    )
    each = count // len(outs)
    for index, out in enumerate(outs):
        out[...] = rows[index * each : (index + 1) * each, :].astype(BF16)


def pick_rows(ids, table, pieces):
    count = ids.shape[0] // pieces
    width = table.shape[1]
    return pl.pallas_call(
        pick_kernel,
        out_shape=[jax.ShapeDtypeStruct((count, width), BF16)] * pieces,
        compiler_params=grant(24),
        cost_estimate=cost(2 * ids.shape[0] * table.shape[0] * width, 2 * table.size),
        name="pick_rows",
    )(ids, table)


def residual_kernel(*refs):
    slot_ref, own_ref = refs[0:2]
    pieces = refs[2:-2]
    out_ref, table = refs[-2:]
    each = pieces[0].shape[0]
    for index, piece in enumerate(pieces):
        table[index * each : (index + 1) * each, :] = piece[...].astype(F32)
    count, slots = own_ref.shape[0], table.shape[0]
    wanted = slot_ref[...] == lax.broadcasted_iota(jnp.int32, (count, slots), 1)
    chosen = lax.dot_general(
        wanted.astype(F32).astype(BF16), table[...].astype(BF16), NN, preferred_element_type=F32
    )
    out_ref[...] = (own_ref[...].astype(F32) - chosen).astype(BF16)


def subtract_rows(slots, own, pieces):
    return pl.pallas_call(
        residual_kernel,
        out_shape=jax.ShapeDtypeStruct(own.shape, BF16),
        scratch_shapes=[pltpu.VMEM((len(pieces) * pieces[0].shape[0], own.shape[1]), F32)],
        compiler_params=grant(16),
        name="subtract_rows",
    )(slots, own, *pieces)


def swap(value, axis, key):
    count = lax.axis_size(axis)
    return lax.ppermute(value, axis, [(i, i ^ key) for i in range(count)])


def everywhere(value, axis, step=1):
    return [value] + [swap(value, axis, key) for key in range(step, lax.axis_size(axis), step)]


def after(value, *others):
    return lax.optimization_barrier((value,) + others)[0]


def on_device(vectors, centroids, assignment):
    row_count, width = vectors.shape
    list_count = centroids.shape[0]
    data_count = lax.axis_size("dp")
    owner_count = lax.axis_size("cent")
    me = lax.axis_index("cent")
    place = jnp.stack([lax.axis_index("dp"), me]).astype(jnp.int32)
    send_count = row_count // owner_count
    capacity = max(2, 2 * send_count // owner_count)
    slot_count = owner_count * capacity
    ratio = row_count * data_count / (list_count * owner_count)
    log_mass = math.log(ratio)

    own = lax.dynamic_slice_in_dim(vectors, me * send_count, send_count, 0)
    keys = jnp.bitwise_xor(assignment // list_count, me)
    local_ids = assignment % list_count
    positions = jnp.arange(send_count, dtype=jnp.int32)
    earlier_same = (keys[:, None] == keys[None, :]) & (positions[None, :] < positions[:, None])
    slots = keys * capacity + jnp.sum(earlier_same.astype(jnp.int32), axis=1)
    picked = slots[:, None] == jnp.arange(row_count, dtype=jnp.int32)[None, :]
    outgoing_ids = jnp.sum(jnp.where(picked, local_ids[:, None], 0), axis=0)
    ids_row = outgoing_ids.astype(F32)[None, :]

    arriving = [swap(own, "dp", 1)]
    logits, stats = logits_and_stats(vectors, centroids)
    scaled, own_stats, first_column = first_rows(
        logits, ids_row, everywhere(stats, "dp"), log_mass
    )
    halves = []

    def across(piece, *ready):
        piece = after(piece, *ready)
        return jnp.concatenate(everywhere(piece, "cent", 2), axis=0)

    arriving += [swap(after(own, stats), "dp", key) for key in range(2, data_count)]
    half = across(arriving[0], stats)
    partner = swap(own_stats, "cent", 1)
    pair = jnp.concatenate(
        join_pairs([own_stats, partner]) + (own_stats[2:3], partner[2:3]), axis=0
    )
    parts = everywhere(pair, "cent", 2)
    used = slot_count
    rows_of = [part[2 + key : 3 + key, :used] for part in parts for key in range(2)]
    arrived = jnp.concatenate(
        [
            rows_of[key][0, key * capacity : (key + 1) * capacity]
            for key in range(owner_count)
        ]
    ).astype(jnp.int32)

    peak = None
    column = first_column
    for turn in range(ITERS - 1):
        if turn == 0:
            sums, peak = column_sums(scaled, own_stats, parts)
        else:
            (sums,) = column_sums(scaled, own_stats, parts, peak)
        halves += [half, swap(after(half, sums), "cent", 1)]
        if turn + 1 < data_count - 1:
            half = across(arriving[turn + 1], sums)
        sums, column = row_sums(
            scaled, first_column, own_stats, peak, everywhere(sums, "dp"), ratio
        )
        parts = everywhere(sums + swap(sums, "cent", 1), "cent", 2)
    row = -(peak + jnp.log(tree(parts, jnp.add)))
    for turn in range(ITERS - 1, data_count - 1):
        if turn > ITERS - 1:
            half = across(arriving[turn], sums)
        halves += [half, swap(half, "cent", 1)]

    updated = new_centroids(
        place, centroids, column, everywhere(row, "dp"), vectors, halves, owner_count
    )
    pieces = pick_rows(arrived[:, None], updated, owner_count)
    pieces = [pieces[0]] + [
        swap(pieces[key], "cent", key) for key in range(1, owner_count)
    ]
    residuals = subtract_rows(slots[:, None], own, pieces)
    return (updated, row.reshape(row_count), column.reshape(list_count), residuals)


def solution(mesh):
    in_specs = (P("dp", None), P("cent", None), P(("dp", "cent")))
    out_specs = (P("cent", None), P("dp"), P("cent"), P(("dp", "cent"), None))
    return jax.shard_map(
        on_device, mesh=mesh, in_specs=in_specs, out_specs=out_specs, check_vma=False
    )
```

```python
import functools
import math

import jax
import jax.numpy as jnp
from jax import lax
from jax.experimental import pallas as pl
from jax.experimental.pallas import tpu as pltpu
from jax.sharding import PartitionSpec as P


ITERS = 3


F32 = jnp.float32
BF16 = jnp.bfloat16
NT = (((1,), (1,)), ((), ()))
NN = (((1,), (0,)), ((), ()))
MIB = 1 << 20


def cost(flops, moved, exps=0):
    return pl.CostEstimate(flops=int(flops), bytes_accessed=int(moved), transcendentals=int(exps))


def grant(mib):
    return pltpu.CompilerParams(vmem_limit_bytes=mib * MIB)


def tree(parts, join):
    while len(parts) > 1:
        parts = [join(parts[k], parts[k + 1]) for k in range(0, len(parts), 2)]
    return parts[0]


def join_pairs(parts):
    peak = tree([part[0:1] for part in parts], jnp.maximum)
    total = tree([part[1:2] * jnp.exp(part[0:1] - peak) for part in parts], jnp.add)
    return peak, total


def in_hbm(value):
    return pltpu.with_memory_space_constraint(value, pltpu.HBM)


def in_vmem(value):
    return pltpu.with_memory_space_constraint(value, pltpu.VMEM)


def whole(shape):
    return pl.BlockSpec(shape, lambda *_: (0,) * len(shape))


def logits_kernel(v_ref, c_ref, l_ref, stat_ref, *, chunk):
    doubled = c_ref[...] * 2
    rows = v_ref.shape[0]
    peak, total = None, None
    for start in range(0, rows, chunk):
        part = lax.dot_general(
            v_ref[start : start + chunk, :], doubled, NT, preferred_element_type=F32
        )
        l_ref[start : start + chunk, :] = part
        part_peak = jnp.max(part, axis=0, keepdims=True)
        higher = part_peak if peak is None else jnp.maximum(peak, part_peak)
        part_total = jnp.sum(jnp.exp(part - higher), axis=0, keepdims=True)
        total = part_total if peak is None else total * jnp.exp(peak - higher) + part_total
        peak = higher
    stat_ref[0:1, :] = peak
    stat_ref[1:2, :] = total


def logits_and_stats(vectors, centroids):
    rows, width = vectors.shape
    lists = centroids.shape[0]
    tile = min(512, lists)
    return pl.pallas_call(
        functools.partial(logits_kernel, chunk=min(256, rows)),
        grid=(lists // tile,),
        in_specs=[whole((rows, width)), pl.BlockSpec((tile, width), lambda j: (j, 0))],
        out_specs=[
            pl.BlockSpec((rows, tile), lambda j: (0, j)),
            pl.BlockSpec((2, tile), lambda j: (0, j)),
        ],
        out_shape=[
            pltpu.VMEM((rows, lists), F32),
            jax.ShapeDtypeStruct((2, lists), F32),
        ],
        compiler_params=grant(24),
        cost_estimate=cost(2 * rows * lists * width, 4 * rows * lists, rows * lists),
        name="logits_stats",
    )(in_hbm(vectors), in_hbm(centroids))


def first_rows_kernel(*refs, parts, log_mass, group):
    l_ref, ids_ref = refs[0:2]
    stats = refs[2 : 2 + parts]
    m_ref, stat_ref, col_ref, peaks, totals = refs[2 + parts :]

    @pl.when(pl.program_id(0) == 0)
    def _():
        peak, total = join_pairs([part[...] for part in stats])
        col_ref[...] = log_mass - (peak + jnp.log(total))

    tile = l_ref.shape[0]

    def some(step, carry):
        rows = pl.ds(pl.multiple_of(step * group, group), group)
        shifted = l_ref[rows, :] + col_ref[...]
        peak = jnp.max(shifted, axis=1, keepdims=True)
        scaled = jnp.exp(shifted - peak)
        m_ref[rows, :] = scaled.astype(BF16)
        peaks[rows, :] = jnp.broadcast_to(peak, (group, 128))
        totals[rows, :] = jnp.broadcast_to(jnp.sum(scaled, axis=1, keepdims=True), (group, 128))
        return carry

    lax.fori_loop(0, tile // group, some, 0, unroll=4)
    stat_ref[0:1, :] = jnp.transpose(peaks[...])[0:1, :]
    stat_ref[1:2, :] = jnp.transpose(totals[...])[0:1, :]
    stat_ref[2:3, :] = ids_ref[...]


def first_rows(logits, ids, stats, log_mass):
    rows, lists = logits.shape
    tile = min(256, rows)
    return pl.pallas_call(
        functools.partial(first_rows_kernel, parts=len(stats), log_mass=log_mass, group=16),
        grid=(rows // tile,),
        in_specs=[
            pl.BlockSpec((tile, lists), lambda i: (i, 0)),
            pl.BlockSpec((1, tile), lambda i: (0, i)),
        ]
        + [whole((2, lists))] * len(stats),
        out_specs=[
            pl.BlockSpec((tile, lists), lambda i: (i, 0)),
            pl.BlockSpec((3, tile), lambda i: (0, i)),
            whole((1, lists)),
        ],
        out_shape=[
            pltpu.VMEM((rows, lists), BF16),
            jax.ShapeDtypeStruct((3, rows), F32),
            jax.ShapeDtypeStruct((1, lists), F32),
        ],
        scratch_shapes=[pltpu.VMEM((tile, 128), F32), pltpu.VMEM((tile, 128), F32)],
        compiler_params=grant(16),
        cost_estimate=cost(4 * rows * lists, 6 * rows * lists, rows * lists),
        name="first_rows",
    )(in_vmem(logits), ids, *stats)


def store_parts(where, value):
    head = value.astype(BF16)
    rest = value - head.astype(F32)
    middle = rest.astype(BF16)
    last = (rest - middle.astype(F32)).astype(BF16)
    zero = jnp.zeros((5, value.shape[1]), BF16)
    where[...] = jnp.concatenate([head, middle, last, zero], axis=0)


def add_parts(sums):
    return (sums[2:3] + sums[1:2]) + sums[0:1]


def column_sum_kernel(*refs, parts, first):
    m_ref, own_ref = refs[0:2]
    stats = refs[2 : 2 + parts]
    if first:
        out_ref, peak_ref, _, weights = refs[2 + parts :]
    else:
        peak_ref = refs[2 + parts]
        out_ref, _, weights = refs[3 + parts :]

    @pl.when(pl.program_id(0) == 0)
    def _():
        if first:
            peak, total = join_pairs([part[...] for part in stats])
            peak_ref[...] = peak
        else:
            peak = peak_ref[...]
            total = tree([part[...] for part in stats], jnp.add)
        store_parts(weights, jnp.exp(own_ref[0:1, :] - (peak + jnp.log(total))))

    out_ref[...] = add_parts(
        lax.dot_general(weights[...], m_ref[...], NN, preferred_element_type=F32)
    )


def column_sums(scaled, own, stats, peak=None):
    rows, lists = scaled.shape
    tile = min(512, lists)
    first = peak is None
    row = whole((1, rows))
    kept = pl.BlockSpec(memory_space=pl.ANY)
    out_specs = [pl.BlockSpec((1, tile), lambda j: (0, j))]
    out_shape = [jax.ShapeDtypeStruct((1, lists), F32)]
    return pl.pallas_call(
        functools.partial(column_sum_kernel, parts=len(stats), first=first),
        grid=(lists // tile,),
        in_specs=[pl.BlockSpec((rows, tile), lambda j: (0, j)), whole(own.shape)]
        + [whole(stats[0].shape)] * len(stats)
        + ([] if first else [row]),
        out_specs=out_specs + ([row] if first else []) + [kept],
        out_shape=out_shape
        + ([jax.ShapeDtypeStruct((1, rows), F32)] if first else [])
        + [pltpu.VMEM(scaled.shape, scaled.dtype)],
        input_output_aliases={0: 2 if first else 1},
        scratch_shapes=[pltpu.VMEM((8, rows), BF16)],
        compiler_params=grant(16),
        cost_estimate=cost(16 * rows * lists, 2 * rows * lists),
        name="column_sums",
    )(in_vmem(scaled), own, *stats, *([] if first else [peak]))


def row_sum_kernel(*refs, parts, ratio, log_mass):
    m_ref, first_ref, own_ref, peak_ref = refs[0:4]
    stats = refs[4 : 4 + parts]
    out_ref, col_ref, _, weights = refs[4 + parts :]

    @pl.when(pl.program_id(0) == 0)
    def _():
        total = tree([part[...] for part in stats], jnp.add)
        store_parts(weights, ratio / total)
        col_ref[...] = first_ref[...] + (log_mass - jnp.log(total))

    sums = add_parts(lax.dot_general(weights[...], m_ref[...], NT, preferred_element_type=F32))
    out_ref[...] = sums * jnp.exp(own_ref[0:1, :] - peak_ref[...])


def row_sums(scaled, first_column, own, peak, stats, ratio):
    rows, lists = scaled.shape
    tile = min(512, rows)
    column = whole((1, lists))
    return pl.pallas_call(
        functools.partial(
            row_sum_kernel, parts=len(stats), ratio=ratio, log_mass=math.log(ratio)
        ),
        grid=(rows // tile,),
        in_specs=[
            pl.BlockSpec((tile, lists), lambda i: (i, 0)),
            column,
            pl.BlockSpec((own.shape[0], tile), lambda i: (0, i)),
            pl.BlockSpec((1, tile), lambda i: (0, i)),
        ]
        + [column] * len(stats),
        out_specs=[
            pl.BlockSpec((1, tile), lambda i: (0, i)),
            column,
            pl.BlockSpec(memory_space=pl.ANY),
        ],
        out_shape=[
            jax.ShapeDtypeStruct((1, rows), F32),
            jax.ShapeDtypeStruct((1, lists), F32),
            pltpu.VMEM(scaled.shape, scaled.dtype),
        ],
        input_output_aliases={0: 2},
        scratch_shapes=[pltpu.VMEM((8, lists), BF16)],
        compiler_params=grant(16),
        cost_estimate=cost(16 * rows * lists, 2 * rows * lists),
        name="row_sums",
    )(in_vmem(scaled), first_column, own, peak, *stats)


def plan_kernel(*refs, planes, owners, depth):
    place_ref, c_ref, col_ref = refs[0:3]
    rows_in = refs[3 : 3 + planes]
    own_ref = refs[3 + planes]
    halves = refs[4 + planes : 4 + planes + 2 * (planes - 1)]
    ids_ref, out_ref = refs[4 + planes + 2 * (planes - 1) : 6 + planes + 2 * (planes - 1)]
    picked = refs[6 + planes + 2 * (planes - 1) : -6]
    held, row_all, acc, mass, chosen, sems = refs[-6:]
    tile = c_ref.shape[0]
    count = own_ref.shape[0]
    piece = count // owners
    plane, owner = place_ref[0], place_ref[1]

    def block(index):
        return pl.ds(pl.multiple_of(index * count, count), count)

    @pl.when(pl.program_id(0) == 0)
    def _():
        pltpu.make_async_copy(own_ref, held.at[block(plane)], sems.at[0]).start()
        row_all[pl.ds(plane, 1), :] = rows_in[0][...]
        for key in range(1, planes):
            other = plane ^ key
            row_all[pl.ds(other, 1), :] = rows_in[key][...]
            for index in range(owners):
                source = halves[2 * (key - 1) + index // (owners // 2)]
                at = (index % (owners // 2)) * piece
                slot = 2 * (index % (owners // 2)) + index // (owners // 2)
                start = pl.multiple_of(other * count + (owner ^ slot) * piece, piece)
                pltpu.make_async_copy(
                    source.at[pl.ds(at, piece)], held.at[pl.ds(start, piece)], sems.at[key]
                ).start()

    doubled = c_ref[...] * 2
    column = jnp.transpose(jnp.broadcast_to(col_ref[...], (128, tile)))[:, 0:1]
    steps = planes * count // depth

    def logits(step):
        here = held[step * depth : (step + 1) * depth, :]
        return lax.dot_general(doubled, here, NT, preferred_element_type=F32)

    @pl.when(pl.program_id(0) == 0)
    def _():
        for key in range(planes):
            pltpu.make_async_copy(held.at[block(key)], held.at[block(key)], sems.at[key]).wait()

    ready = logits(0)
    for step in range(steps):
        following = logits(step + 1) if step + 1 < steps else None
        start = step * depth
        row = row_all[start // count : start // count + 1, start % count : start % count + depth]
        plan = jnp.exp(ready + row + column).astype(BF16)
        part = lax.dot_general(
            plan, held[start : start + depth, :], NN, preferred_element_type=F32
        )
        wide = plan.astype(F32)
        sums = wide[:, 0:128]
        for lane in range(128, depth, 128):
            sums = sums + wide[:, lane : lane + 128]
        acc[...] = part if step == 0 else acc[...] + part
        mass[...] = sums if step == 0 else mass[...] + sums
        ready = following
    fresh = (acc[...] / jnp.sum(mass[...], axis=1, keepdims=True)).astype(BF16)
    out_ref[...] = fresh
    turn = pl.program_id(0)
    slots = ids_ref.shape[0]
    lanes = lax.broadcasted_iota(jnp.int32, (slots, tile), 1) + turn * tile
    wanted = (ids_ref[...] == lanes).astype(F32).astype(BF16)
    some = lax.dot_general(wanted, fresh, NN, preferred_element_type=F32)

    @pl.when(turn == 0)
    def _():
        chosen[...] = some

    @pl.when(turn > 0)
    def _():
        chosen[...] += some

    @pl.when(turn == pl.num_programs(0) - 1)
    def _():
        each = slots // len(picked)
        for index, piece_ref in enumerate(picked):
            piece_ref[...] = chosen[index * each : (index + 1) * each, :].astype(BF16)


def new_centroids(place, centroids, column, rows, own, halves, ids, owners):
    count, width = own.shape
    lists = centroids.shape[0]
    planes = len(rows)
    tile, depth = min(256, lists), min(1024, count)
    anywhere = pl.BlockSpec(memory_space=pl.ANY)
    total = planes * count
    return pl.pallas_call(
        functools.partial(plan_kernel, planes=planes, owners=owners, depth=depth),
        grid=(lists // tile,),
        in_specs=[
            pl.BlockSpec(memory_space=pltpu.SMEM),
            pl.BlockSpec((tile, width), lambda j: (j, 0)),
            pl.BlockSpec((1, tile), lambda j: (0, j)),
        ]
        + [whole((1, count))] * planes
        + [anywhere] * (1 + len(halves))
        + [whole(ids.shape)],
        out_specs=[pl.BlockSpec((tile, width), lambda j: (j, 0))]
        + [whole((ids.shape[0] // owners, width))] * owners,
        out_shape=[jax.ShapeDtypeStruct((lists, width), BF16)]
        + [jax.ShapeDtypeStruct((ids.shape[0] // owners, width), BF16)] * owners,
        scratch_shapes=[
            pltpu.VMEM((total, width), BF16),
            pltpu.VMEM((max(8, planes), count), F32),
            pltpu.VMEM((tile, width), F32),
            pltpu.VMEM((tile, 128), F32),
            pltpu.VMEM((ids.shape[0], width), F32),
            pltpu.SemaphoreType.DMA((planes,)),
        ],
        compiler_params=grant(40),
        cost_estimate=cost(4 * total * lists * width, 2 * total * width, total * lists),
        name="new_centroids",
    )(place, in_hbm(centroids), column, *rows, in_hbm(own), *halves, ids)


def residual_kernel(*refs):
    slot_ref, own_ref = refs[0:2]
    pieces = refs[2:-2]
    out_ref, table = refs[-2:]
    each = pieces[0].shape[0]
    for index, piece in enumerate(pieces):
        table[index * each : (index + 1) * each, :] = piece[...].astype(F32)
    count, slots = own_ref.shape[0], table.shape[0]
    wanted = slot_ref[...] == lax.broadcasted_iota(jnp.int32, (count, slots), 1)
    chosen = lax.dot_general(
        wanted.astype(F32).astype(BF16), table[...].astype(BF16), NN, preferred_element_type=F32
    )
    out_ref[...] = (own_ref[...].astype(F32) - chosen).astype(BF16)


def subtract_rows(slots, own, pieces):
    return pl.pallas_call(
        residual_kernel,
        out_shape=jax.ShapeDtypeStruct(own.shape, BF16),
        scratch_shapes=[pltpu.VMEM((len(pieces) * pieces[0].shape[0], own.shape[1]), F32)],
        compiler_params=grant(16),
        name="subtract_rows",
    )(slots, own, *pieces)


def swap(value, axis, key):
    count = lax.axis_size(axis)
    return lax.ppermute(value, axis, [(i, i ^ key) for i in range(count)])


def everywhere(value, axis, step=1):
    return [value] + [swap(value, axis, key) for key in range(step, lax.axis_size(axis), step)]


def after(value, *others):
    return lax.optimization_barrier((value,) + others)[0]


def step_on_device(vectors, centroids, assignment):
    row_count, _ = vectors.shape
    list_count = centroids.shape[0]
    data_count = lax.axis_size("dp")
    owner_count = lax.axis_size("cent")
    me = lax.axis_index("cent")
    place = jnp.stack([lax.axis_index("dp"), me]).astype(jnp.int32)
    send_count = row_count // owner_count
    capacity = max(2, 2 * send_count // owner_count)
    slot_count = owner_count * capacity
    ratio = row_count * data_count / (list_count * owner_count)
    log_mass = math.log(ratio)

    own = lax.dynamic_slice_in_dim(vectors, me * send_count, send_count, 0)
    keys = jnp.bitwise_xor(assignment // list_count, me)
    local_ids = assignment % list_count
    positions = jnp.arange(send_count, dtype=jnp.int32)
    earlier_same = (keys[:, None] == keys[None, :]) & (positions[None, :] < positions[:, None])
    slots = keys * capacity + jnp.sum(earlier_same.astype(jnp.int32), axis=1)
    picked = slots[:, None] == jnp.arange(row_count, dtype=jnp.int32)[None, :]
    outgoing_ids = jnp.sum(jnp.where(picked, local_ids[:, None], 0), axis=0)
    ids_row = outgoing_ids.astype(F32)[None, :]

    def across(piece, *ready):
        return everywhere(after(piece, *ready), "cent", 2)

    def partners(pieces):
        half = jnp.concatenate(pieces, axis=0)
        return [half, swap(half, "cent", 1)]

    arriving = [swap(own, "dp", 1)]
    logits, stats = logits_and_stats(vectors, centroids)
    parts = everywhere(stats, "dp")
    if data_count > 2:
        arriving.append(swap(after(own, stats), "dp", 2))
    moved = across(arriving[0], stats)
    scaled, own_stats, first_column = first_rows(logits, ids_row, parts, log_mass)
    partner = swap(own_stats, "cent", 1)
    pair = jnp.concatenate(
        join_pairs([own_stats, partner]) + (own_stats[2:3], partner[2:3]), axis=0
    )
    parts = everywhere(pair, "cent", 2)
    rows_of = [part[2 + key : 3 + key, :slot_count] for part in parts for key in range(2)]
    arrived = jnp.concatenate(
        [rows_of[key][0, key * capacity : (key + 1) * capacity] for key in range(owner_count)]
    ).astype(jnp.int32)

    peak = None
    halves = []
    for turn in range(1, ITERS):
        halves += partners(moved)
        moved = across(arriving[turn], pair)
        if turn == 1:
            sums, peak, scaled = column_sums(scaled, own_stats, parts)
        else:
            sums, scaled = column_sums(scaled, own_stats, parts, peak)
        parts = everywhere(sums, "dp")
        if turn == 1:
            for key in range(3, data_count):
                arriving.append(swap(after(own, sums), "dp", key))
        sums, column, scaled = row_sums(scaled, first_column, own_stats, peak, parts, ratio)
        partner = swap(sums, "cent", 1)
        pair = sums + partner
        parts = everywhere(pair, "cent", 2)
    halves += partners(moved)
    for turn in range(ITERS, data_count - 1):
        halves += partners(across(arriving[turn]))
    row = -(peak + jnp.log(tree(parts, jnp.add)))

    rows = everywhere(row, "dp")
    updated, *pieces = new_centroids(
        place, centroids, column, rows, vectors, halves, arrived[:, None], owner_count
    )
    pieces = [pieces[0]] + [swap(pieces[key], "cent", key) for key in range(1, owner_count)]
    residuals = subtract_rows(slots[:, None], own, pieces)
    return (updated, row.reshape(row_count), column.reshape(list_count), residuals)


def solution(mesh):
    in_specs = (P("dp", None), P("cent", None), P(("dp", "cent")))
    out_specs = (P("cent", None), P("dp"), P("cent"), P(("dp", "cent"), None))
    return jax.shard_map(
        step_on_device, mesh=mesh, in_specs=in_specs, out_specs=out_specs, check_vma=False
    )
```

```python
import functools
import math

import jax
import jax.numpy as jnp
from jax import lax
from jax.experimental import pallas as pl
from jax.experimental.pallas import tpu as pltpu
from jax.sharding import PartitionSpec as P


ITERS = 3


F32 = jnp.float32
BF16 = jnp.bfloat16
NT = (((1,), (1,)), ((), ()))
NN = (((1,), (0,)), ((), ()))
MIB = 1 << 20
OWN_TILE = 1024


def cost(flops, moved, exps=0):
    return pl.CostEstimate(flops=int(flops), bytes_accessed=int(moved), transcendentals=int(exps))


def grant(mib):
    return pltpu.CompilerParams(vmem_limit_bytes=mib * MIB)


def tree(parts, join):
    while len(parts) > 1:
        parts = [join(parts[k], parts[k + 1]) for k in range(0, len(parts), 2)]
    return parts[0]


def join_pairs(parts):
    peak = tree([part[0:1] for part in parts], jnp.maximum)
    total = tree([part[1:2] * jnp.exp(part[0:1] - peak) for part in parts], jnp.add)
    return peak, total


def in_hbm(value):
    return pltpu.with_memory_space_constraint(value, pltpu.HBM)


def in_vmem(value):
    return pltpu.with_memory_space_constraint(value, pltpu.VMEM)


def whole(shape):
    return pl.BlockSpec(shape, lambda *_: (0,) * len(shape))


def logits_kernel(v_ref, c_ref, l_ref, stat_ref, *, chunk):
    doubled = c_ref[...] * 2
    rows = v_ref.shape[0]
    peak, total = None, None
    for start in range(0, rows, chunk):
        part = lax.dot_general(
            v_ref[start : start + chunk, :], doubled, NT, preferred_element_type=F32
        )
        l_ref[start : start + chunk, :] = part
        part_peak = jnp.max(part, axis=0, keepdims=True)
        higher = part_peak if peak is None else jnp.maximum(peak, part_peak)
        part_total = jnp.sum(jnp.exp(part - higher), axis=0, keepdims=True)
        total = part_total if peak is None else total * jnp.exp(peak - higher) + part_total
        peak = higher
    stat_ref[0:1, :] = peak
    stat_ref[1:2, :] = total


def logits_and_stats(vectors, centroids):
    rows, width = vectors.shape
    lists = centroids.shape[0]
    tile = min(512, lists)
    return pl.pallas_call(
        functools.partial(logits_kernel, chunk=min(256, rows)),
        grid=(lists // tile,),
        in_specs=[whole((rows, width)), pl.BlockSpec((tile, width), lambda j: (j, 0))],
        out_specs=[
            pl.BlockSpec((rows, tile), lambda j: (0, j)),
            pl.BlockSpec((2, tile), lambda j: (0, j)),
        ],
        out_shape=[
            pltpu.VMEM((rows, lists), F32),
            jax.ShapeDtypeStruct((2, lists), F32),
        ],
        compiler_params=grant(24),
        cost_estimate=cost(2 * rows * lists * width, 4 * rows * lists, rows * lists),
        name="logits_stats",
    )(in_hbm(vectors), in_hbm(centroids))


def first_rows_kernel(*refs, parts, log_mass, group):
    l_ref, ids_ref = refs[0:2]
    stats = refs[2 : 2 + parts]
    m_ref, stat_ref, col_ref, spare_ref, peaks, totals = refs[2 + parts :]

    @pl.when(pl.program_id(0) == 0)
    def _():
        peak, total = join_pairs([part[...] for part in stats])
        col_ref[...] = log_mass - (peak + jnp.log(total))

    tile = l_ref.shape[0]

    def some(step, carry):
        rows = pl.ds(pl.multiple_of(step * group, group), group)
        shifted = l_ref[rows, :] + col_ref[...]
        peak = jnp.max(shifted, axis=1, keepdims=True)
        scaled = jnp.exp(shifted - peak)
        rounded = scaled.astype(BF16)
        m_ref[rows, :] = rounded
        spare_ref[rows, :] = rounded
        peaks[rows, :] = jnp.broadcast_to(peak, (group, 128))
        totals[rows, :] = jnp.broadcast_to(jnp.sum(scaled, axis=1, keepdims=True), (group, 128))
        return carry

    lax.fori_loop(0, tile // group, some, 0, unroll=4)
    stat_ref[0:1, :] = jnp.transpose(peaks[...])[0:1, :]
    stat_ref[1:2, :] = jnp.transpose(totals[...])[0:1, :]
    stat_ref[2:3, :] = ids_ref[...]


def first_rows(logits, ids, stats, log_mass):
    rows, lists = logits.shape
    tile = min(512, rows)
    return pl.pallas_call(
        functools.partial(first_rows_kernel, parts=len(stats), log_mass=log_mass, group=32),
        grid=(rows // tile,),
        in_specs=[
            pl.BlockSpec((tile, lists), lambda i: (i, 0)),
            pl.BlockSpec((1, tile), lambda i: (0, i)),
        ]
        + [whole((2, lists))] * len(stats),
        out_specs=[
            pl.BlockSpec((tile, lists), lambda i: (i, 0)),
            pl.BlockSpec((3, tile), lambda i: (0, i)),
            whole((1, lists)),
            pl.BlockSpec((tile, lists), lambda i: (i, 0)),
        ],
        out_shape=[
            pltpu.VMEM((rows, lists), BF16),
            jax.ShapeDtypeStruct((3, rows), F32),
            jax.ShapeDtypeStruct((1, lists), F32),
            pltpu.HBM((rows, lists), BF16),
        ],
        scratch_shapes=[pltpu.VMEM((tile, 128), F32), pltpu.VMEM((tile, 128), F32)],
        compiler_params=grant(24),
        cost_estimate=cost(4 * rows * lists, 6 * rows * lists, rows * lists),
        name="first_rows",
    )(in_vmem(logits), ids, *stats)


def store_parts(where, value):
    head = value.astype(BF16)
    rest = value - head.astype(F32)
    middle = rest.astype(BF16)
    last = (rest - middle.astype(F32)).astype(BF16)
    zero = jnp.zeros((5, value.shape[1]), BF16)
    where[...] = jnp.concatenate([head, middle, last, zero], axis=0)


def add_parts(sums):
    return (sums[2:3] + sums[1:2]) + sums[0:1]


def column_sum_kernel(*refs, parts, first):
    m_ref, own_ref = refs[0:2]
    stats = refs[2 : 2 + parts]
    weights = refs[-1]
    if first:
        out_ref, peak_ref = refs[2 + parts : 4 + parts]
    else:
        peak_ref, out_ref = refs[2 + parts : 4 + parts]

    @pl.when(pl.program_id(0) == 0)
    def _():
        if first:
            peak, total = join_pairs([part[...] for part in stats])
            peak_ref[...] = peak
        else:
            peak = peak_ref[...]
            total = tree([part[...] for part in stats], jnp.add)
        store_parts(weights, jnp.exp(own_ref[0:1, :] - (peak + jnp.log(total))))

    out_ref[...] = add_parts(
        lax.dot_general(weights[...], m_ref[...], NN, preferred_element_type=F32)
    )


def column_sums(scaled, own, stats, last, peak=None):
    rows, lists = scaled.shape
    tile = min(512, lists)
    first = peak is None
    row = whole((1, rows))
    kept = pl.BlockSpec(memory_space=pl.ANY)
    out_specs = [pl.BlockSpec((1, tile), lambda j: (0, j))]
    out_shape = [jax.ShapeDtypeStruct((1, lists), F32)]
    return pl.pallas_call(
        functools.partial(column_sum_kernel, parts=len(stats), first=first),
        grid=(lists // tile,),
        in_specs=[pl.BlockSpec((rows, tile), lambda j: (0, j)), whole(own.shape)]
        + [whole(stats[0].shape)] * len(stats)
        + ([] if first else [row]),
        out_specs=out_specs + ([row] if first else []) + ([] if last else [kept]),
        out_shape=out_shape
        + ([jax.ShapeDtypeStruct((1, rows), F32)] if first else [])
        + ([] if last else [pltpu.VMEM(scaled.shape, scaled.dtype)]),
        input_output_aliases={} if last else {0: 2 if first else 1},
        scratch_shapes=[pltpu.VMEM((8, rows), BF16)],
        compiler_params=grant(16),
        cost_estimate=cost(16 * rows * lists, 2 * rows * lists),
        name="column_sums",
    )(in_vmem(scaled), own, *stats, *([] if first else [peak]))


def row_sum_kernel(*refs, parts, ratio, log_mass):
    m_ref, first_ref, own_ref, peak_ref = refs[0:4]
    stats = refs[4 : 4 + parts]
    out_ref, col_ref, weights = refs[4 + parts], refs[5 + parts], refs[-1]

    @pl.when(pl.program_id(0) == 0)
    def _():
        total = tree([part[...] for part in stats], jnp.add)
        store_parts(weights, ratio / total)
        col_ref[...] = first_ref[...] + (log_mass - jnp.log(total))

    sums = add_parts(lax.dot_general(weights[...], m_ref[...], NT, preferred_element_type=F32))
    out_ref[...] = sums * jnp.exp(own_ref[0:1, :] - peak_ref[...])


def row_sums(scaled, first_column, own, peak, stats, ratio, last):
    rows, lists = scaled.shape
    tile = min(512, rows)
    column = whole((1, lists))
    return pl.pallas_call(
        functools.partial(
            row_sum_kernel, parts=len(stats), ratio=ratio, log_mass=math.log(ratio)
        ),
        grid=(rows // tile,),
        in_specs=[
            pl.BlockSpec((tile, lists), lambda i: (i, 0)),
            column,
            pl.BlockSpec((own.shape[0], tile), lambda i: (0, i)),
            pl.BlockSpec((1, tile), lambda i: (0, i)),
        ]
        + [column] * len(stats),
        out_specs=[
            pl.BlockSpec((1, tile), lambda i: (0, i)),
            column,
        ]
        + ([] if last else [pl.BlockSpec(memory_space=pl.ANY)]),
        out_shape=[
            jax.ShapeDtypeStruct((1, rows), F32),
            jax.ShapeDtypeStruct((1, lists), F32),
        ]
        + ([] if last else [pltpu.VMEM(scaled.shape, scaled.dtype)]),
        input_output_aliases={} if last else {0: 2},
        scratch_shapes=[pltpu.VMEM((8, lists), BF16)],
        compiler_params=grant(16),
        cost_estimate=cost(16 * rows * lists, 2 * rows * lists),
        name="row_sums",
    )(in_hbm(scaled) if last else in_vmem(scaled), first_column, own, peak, *stats)


def block_sums(blocks):
    flat = [(index, item) for index, block in enumerate(blocks) for item in block]

    def logits(item):
        return lax.dot_general(item[0], item[2](), NT, preferred_element_type=F32)

    found = [None] * len(blocks)
    ready = logits(flat[0][1])
    for place, (index, item) in enumerate(flat):
        following = logits(flat[place + 1][1]) if place + 1 < len(flat) else None
        plan = jnp.exp(ready + item[3]() + item[1]).astype(BF16)
        part = lax.dot_general(plan, item[2](), NN, preferred_element_type=F32)
        wide = plan.astype(F32)
        sums = wide[:, 0:128]
        for lane in range(128, wide.shape[1], 128):
            sums = sums + wide[:, lane : lane + 128]
        before = found[index]
        found[index] = (part, sums) if before is None else (before[0] + part, before[1] + sums)
        ready = following
    return found


def chunk(index, depth):
    return slice(index * depth, (index + 1) * depth)


def wide_column(col_ref):
    size = col_ref.shape[1]
    return jnp.transpose(jnp.broadcast_to(col_ref[...], (128, size)))[:, 0:1]


def loads(ref, rows, columns):
    return lambda: ref[rows, columns]


def own_plan_kernel(c_ref, col_ref, v_ref, r_ref, sum_ref, mass_ref, *, depth, part):
    doubled, column = c_ref[...] * 2, wide_column(col_ref)
    every = slice(None)
    parts = [slice(start, start + part) for start in range(0, doubled.shape[0], part)]
    blocks = [
        [
            (
                doubled[here],
                column[here],
                loads(v_ref, chunk(step, depth), every),
                loads(r_ref, every, chunk(step, depth)),
            )
            for step in range(v_ref.shape[0] // depth)
        ]
        for here in parts
    ]
    for here, (total, weight) in zip(parts, block_sums(blocks)):
        sum_ref[here, :] = total
        mass_ref[here, :] = weight


def own_plan(centroids, column, vectors, row):
    count, width = vectors.shape
    lists = centroids.shape[0]
    tile, depth = min(OWN_TILE, lists), min(1024, count)
    return pl.pallas_call(
        functools.partial(own_plan_kernel, depth=depth, part=min(256, lists)),
        grid=(lists // tile,),
        in_specs=[
            pl.BlockSpec((tile, width), lambda j: (j, 0)),
            pl.BlockSpec((1, tile), lambda j: (0, j)),
            whole((count, width)),
            whole((1, count)),
        ],
        out_specs=[
            pl.BlockSpec((tile, width), lambda j: (j, 0)),
            pl.BlockSpec((tile, 128), lambda j: (j, 0)),
        ],
        out_shape=[
            pltpu.HBM((lists, width), F32),
            pltpu.HBM((lists, 128), F32),
        ],
        compiler_params=grant(40),
        cost_estimate=cost(4 * count * lists * width, 4 * lists * width, count * lists),
        name="own_plan",
    )(in_hbm(centroids), column, in_hbm(vectors), row)


def plan_kernel(*refs, planes, owners, depth):
    others = planes - 1
    place_ref, c_ref, col_ref, sum_ref, mass_ref, ids_ref = refs[0:6]
    rows_in = refs[6 : 6 + others]
    halves = refs[6 + others : 6 + 3 * others]
    out_ref = refs[6 + 3 * others]
    picked = refs[7 + 3 * others : -3]
    held, chosen, sems = refs[-3:]
    tile = c_ref.shape[0]
    count = held.shape[0] // others
    piece = count // owners
    turn = pl.program_id(0)

    def copies(key):
        for index in range(owners):
            source = halves[2 * (key - 1) + index // (owners // 2)]
            at = (index % (owners // 2)) * piece
            slot = 2 * (index % (owners // 2)) + index // (owners // 2)
            start = (key - 1) * count + (place_ref[0] ^ slot) * piece
            yield pltpu.make_async_copy(
                source.at[pl.ds(at, piece)],
                held.at[pl.ds(pl.multiple_of(start, piece), piece)],
                sems.at[key - 1],
            )

    def wait(key):
        here = held.at[pl.ds((key - 1) * count, count)]
        pltpu.make_async_copy(here, here, sems.at[key - 1]).wait()

    def compute():
        doubled, column = c_ref[...] * 2, wide_column(col_ref)
        steps = count // depth
        every = slice(None)
        blocks = [
            [
                (
                    doubled,
                    column,
                    loads(held, chunk((key - 1) * steps + step, depth), every),
                    loads(rows_in[key - 1], every, chunk(step, depth)),
                )
                for step in range(steps)
            ]
            for key in range(1, planes)
        ]
        found = [(sum_ref[...], mass_ref[...])] + block_sums(blocks)
        numerator = tree([item[0] for item in found], jnp.add)
        weight = tree([item[1] for item in found], jnp.add)
        fresh = (numerator / jnp.sum(weight, axis=1, keepdims=True)).astype(BF16)
        out_ref[...] = fresh
        slots = ids_ref.shape[0]
        lanes = lax.broadcasted_iota(jnp.int32, (slots, tile), 1) + turn * tile
        wanted = (ids_ref[...] == lanes).astype(F32).astype(BF16)
        return lax.dot_general(wanted, fresh, NN, preferred_element_type=F32)

    @pl.when(turn == 0)
    def _():
        for key in range(1, planes):
            for copy in copies(key):
                copy.start()
        chosen[...] = jnp.zeros_like(chosen)
        for key in range(1, planes):
            wait(key)

    chosen[...] += compute()

    @pl.when(turn == pl.num_programs(0) - 1)
    def _():
        each = ids_ref.shape[0] // len(picked)
        for index, piece_ref in enumerate(picked):
            piece_ref[...] = chosen[index * each : (index + 1) * each, :].astype(BF16)


def new_centroids(place, centroids, column, sums, masses, ids, rows, halves, owners):
    lists, width = centroids.shape
    others = len(rows)
    count = rows[0].shape[1]
    tile, depth = min(256, lists), min(1024, count)
    total = others * count
    return pl.pallas_call(
        functools.partial(plan_kernel, planes=others + 1, owners=owners, depth=depth),
        grid=(lists // tile,),
        in_specs=[
            pl.BlockSpec(memory_space=pltpu.SMEM),
            pl.BlockSpec((tile, width), lambda j: (j, 0)),
            pl.BlockSpec((1, tile), lambda j: (0, j)),
            pl.BlockSpec((tile, width), lambda j: (j, 0)),
            pl.BlockSpec((tile, 128), lambda j: (j, 0)),
            whole(ids.shape),
        ]
        + [whole((1, count))] * others
        + [pl.BlockSpec(memory_space=pl.ANY)] * len(halves),
        out_specs=[pl.BlockSpec((tile, width), lambda j: (j, 0))]
        + [whole((ids.shape[0] // owners, width))] * owners,
        out_shape=[jax.ShapeDtypeStruct((lists, width), BF16)]
        + [jax.ShapeDtypeStruct((ids.shape[0] // owners, width), BF16)] * owners,
        scratch_shapes=[
            pltpu.VMEM((total, width), BF16),
            pltpu.VMEM((ids.shape[0], width), F32),
            pltpu.SemaphoreType.DMA((others,)),
        ],
        compiler_params=grant(40),
        cost_estimate=cost(4 * total * lists * width, 2 * total * width, total * lists),
        name="new_centroids",
    )(
        place,
        in_hbm(centroids),
        column,
        in_hbm(sums),
        in_hbm(masses),
        ids,
        *rows,
        *[in_hbm(half) for half in halves],
    )


def residual_kernel(*refs):
    slot_ref, own_ref = refs[0:2]
    pieces = refs[2:-2]
    out_ref, table = refs[-2:]
    each = pieces[0].shape[0]
    for index, piece in enumerate(pieces):
        table[index * each : (index + 1) * each, :] = piece[...].astype(F32)
    count, slots = own_ref.shape[0], table.shape[0]
    wanted = slot_ref[...] == lax.broadcasted_iota(jnp.int32, (count, slots), 1)
    chosen = lax.dot_general(
        wanted.astype(F32).astype(BF16), table[...].astype(BF16), NN, preferred_element_type=F32
    )
    out_ref[...] = (own_ref[...].astype(F32) - chosen).astype(BF16)


def subtract_rows(slots, own, pieces):
    return pl.pallas_call(
        residual_kernel,
        out_shape=jax.ShapeDtypeStruct(own.shape, BF16),
        scratch_shapes=[pltpu.VMEM((len(pieces) * pieces[0].shape[0], own.shape[1]), F32)],
        compiler_params=grant(16),
        name="subtract_rows",
    )(slots, own, *pieces)


def join_kernel(*refs):
    pieces, out_ref, sems = refs[:-2], refs[-2], refs[-1]
    each = pieces[0].shape[0]
    moves = [
        pltpu.make_async_copy(piece, out_ref.at[pl.ds(index * each, each)], sems.at[index])
        for index, piece in enumerate(pieces)
    ]
    for move in moves:
        move.start()
    for move in moves:
        move.wait()


def join_pieces(pieces):
    each, width = pieces[0].shape
    anywhere = pl.BlockSpec(memory_space=pl.ANY)
    return pl.pallas_call(
        join_kernel,
        in_specs=[anywhere] * len(pieces),
        out_specs=anywhere,
        out_shape=pltpu.HBM((each * len(pieces), width), pieces[0].dtype),
        scratch_shapes=[pltpu.SemaphoreType.DMA((len(pieces),))],
        compiler_params=grant(4),
        cost_estimate=cost(0, 2 * each * len(pieces) * width),
        name="join_pieces",
    )(*[in_vmem(piece) for piece in pieces])


def swap(value, axis, key):
    count = lax.axis_size(axis)
    return lax.ppermute(value, axis, [(i, i ^ key) for i in range(count)])


def everywhere(value, axis, step=1):
    return [value] + [swap(value, axis, key) for key in range(step, lax.axis_size(axis), step)]


def after(value, *others):
    return lax.optimization_barrier((value,) + others)[0]


def step_on_device(vectors, centroids, assignment):
    row_count, _ = vectors.shape
    list_count = centroids.shape[0]
    data_count = lax.axis_size("dp")
    owner_count = lax.axis_size("cent")
    me = lax.axis_index("cent")
    place = me.astype(jnp.int32)[None]
    send_count = row_count // owner_count
    capacity = max(2, 2 * send_count // owner_count)
    slot_count = owner_count * capacity
    ratio = row_count * data_count / (list_count * owner_count)
    log_mass = math.log(ratio)

    own = lax.dynamic_slice_in_dim(vectors, me * send_count, send_count, 0)
    keys = jnp.bitwise_xor(assignment // list_count, me)
    local_ids = assignment % list_count
    positions = jnp.arange(send_count, dtype=jnp.int32)
    earlier_same = (keys[:, None] == keys[None, :]) & (positions[None, :] < positions[:, None])
    slots = keys * capacity + jnp.sum(earlier_same.astype(jnp.int32), axis=1)
    picked = slots[:, None] == jnp.arange(row_count, dtype=jnp.int32)[None, :]
    outgoing_ids = jnp.sum(jnp.where(picked, local_ids[:, None], 0), axis=0)
    ids_row = outgoing_ids.astype(F32)[None, :]

    def across(piece, *ready):
        return everywhere(after(piece, *ready), "cent", 2)

    def partners(pieces):
        half = join_pieces(pieces)
        return [half, swap(half, "cent", 1)]

    arriving = [swap(own, "dp", 1)]
    logits, stats = logits_and_stats(vectors, centroids)
    parts = everywhere(stats, "dp")
    if data_count > 2:
        arriving.append(swap(after(own, *parts), "dp", 2))
    moved = across(arriving[0], stats)
    scaled, own_stats, first_column, spare = first_rows(logits, ids_row, parts, log_mass)
    partner = swap(own_stats, "cent", 1)
    pair = jnp.concatenate(
        join_pairs([own_stats, partner]) + (own_stats[2:3], partner[2:3]), axis=0
    )
    parts = everywhere(pair, "cent", 2)
    rows_of = [part[2 + key : 3 + key, :slot_count] for part in parts for key in range(2)]
    arrived = jnp.concatenate(
        [rows_of[key][0, key * capacity : (key + 1) * capacity] for key in range(owner_count)]
    ).astype(jnp.int32)

    peak = None
    halves = []
    for turn in range(1, ITERS):
        halves += partners(moved)
        moved = across(arriving[turn], pair)
        last = turn == ITERS - 1
        sums, *kept = column_sums(scaled, own_stats, parts, last, peak)
        peak = kept.pop(0) if turn == 1 else peak
        scaled = scaled if last else kept[0]
        parts = everywhere(sums, "dp")
        if turn == 1:
            for key in range(3, data_count):
                arriving.append(swap(after(own, *parts), "dp", key))
        sums, column, *kept = row_sums(
            spare if last else scaled, first_column, own_stats, peak, parts, ratio, last
        )
        scaled = scaled if last else kept[0]
        partner = swap(sums, "cent", 1)
        pair = sums + partner
        parts = everywhere(pair, "cent", 2)
    halves += partners(moved)
    for turn in range(ITERS, data_count - 1):
        halves += partners(across(arriving[turn]))
    row = -(peak + jnp.log(tree(parts, jnp.add)))

    rows = everywhere(row, "dp")[1:]
    sums, masses = own_plan(centroids, column, vectors, row)
    updated, *pieces = new_centroids(
        place,
        centroids,
        column,
        sums,
        masses,
        arrived[:, None],
        rows,
        halves,
        owner_count,
    )
    pieces = [pieces[0]] + [swap(pieces[key], "cent", key) for key in range(1, owner_count)]
    residuals = subtract_rows(slots[:, None], own, pieces)
    return (updated, row.reshape(row_count), column.reshape(list_count), residuals)


def solution(mesh):
    in_specs = (P("dp", None), P("cent", None), P(("dp", "cent")))
    out_specs = (P("cent", None), P("dp"), P("cent"), P(("dp", "cent"), None))
    return jax.shard_map(
        step_on_device, mesh=mesh, in_specs=in_specs, out_specs=out_specs, check_vma=False
    )
```

```python
import functools
import math

import jax
import jax.numpy as jnp
from jax import lax
from jax.experimental import pallas as pl
from jax.experimental.pallas import tpu as pltpu
from jax.sharding import PartitionSpec as P


ITERS = 3


F32 = jnp.float32
BF16 = jnp.bfloat16
NT = (((1,), (1,)), ((), ()))
NN = (((1,), (0,)), ((), ()))
MIB = 1 << 20
OWN_TILE = 1024


def cost(flops, moved, exps=0):
    return pl.CostEstimate(flops=int(flops), bytes_accessed=int(moved), transcendentals=int(exps))


def grant(mib):
    return pltpu.CompilerParams(vmem_limit_bytes=mib * MIB)


def tree(parts, join):
    while len(parts) > 1:
        parts = [join(parts[k], parts[k + 1]) for k in range(0, len(parts), 2)]
    return parts[0]


def join_pairs(parts):
    peak = tree([part[0:1] for part in parts], jnp.maximum)
    total = tree([part[1:2] * jnp.exp(part[0:1] - peak) for part in parts], jnp.add)
    return peak, total


def in_hbm(value):
    return pltpu.with_memory_space_constraint(value, pltpu.HBM)


def in_vmem(value):
    return pltpu.with_memory_space_constraint(value, pltpu.VMEM)


def whole(shape):
    return pl.BlockSpec(shape, lambda *_: (0,) * len(shape))


def logits_kernel(v_ref, c_ref, l_ref, stat_ref, *, chunk):
    doubled = c_ref[...] * 2
    rows = v_ref.shape[0]
    peak, total = None, None
    for start in range(0, rows, chunk):
        part = lax.dot_general(
            v_ref[start : start + chunk, :], doubled, NT, preferred_element_type=F32
        )
        l_ref[start : start + chunk, :] = part
        part_peak = jnp.max(part, axis=0, keepdims=True)
        higher = part_peak if peak is None else jnp.maximum(peak, part_peak)
        part_total = jnp.sum(jnp.exp(part - higher), axis=0, keepdims=True)
        total = part_total if peak is None else total * jnp.exp(peak - higher) + part_total
        peak = higher
    stat_ref[0:1, :] = peak
    stat_ref[1:2, :] = total


def logits_and_stats(vectors, centroids):
    rows, width = vectors.shape
    lists = centroids.shape[0]
    tile = min(512, lists)
    return pl.pallas_call(
        functools.partial(logits_kernel, chunk=min(256, rows)),
        grid=(lists // tile,),
        in_specs=[whole((rows, width)), pl.BlockSpec((tile, width), lambda j: (j, 0))],
        out_specs=[
            pl.BlockSpec((rows, tile), lambda j: (0, j)),
            pl.BlockSpec((2, tile), lambda j: (0, j)),
        ],
        out_shape=[
            pltpu.VMEM((rows, lists), F32),
            jax.ShapeDtypeStruct((2, lists), F32),
        ],
        compiler_params=grant(24),
        cost_estimate=cost(2 * rows * lists * width, 4 * rows * lists, rows * lists),
        name="logits_stats",
    )(in_hbm(vectors), in_hbm(centroids))


def first_rows_kernel(*refs, parts, log_mass, group):
    l_ref, ids_ref = refs[0:2]
    stats = refs[2 : 2 + parts]
    m_ref, stat_ref, col_ref, peaks, totals = refs[2 + parts :]

    @pl.when(pl.program_id(0) == 0)
    def _():
        peak, total = join_pairs([part[...] for part in stats])
        col_ref[...] = log_mass - (peak + jnp.log(total))

    tile = l_ref.shape[0]

    def some(step, carry):
        rows = pl.ds(pl.multiple_of(step * group, group), group)
        shifted = l_ref[rows, :] + col_ref[...]
        peak = jnp.max(shifted, axis=1, keepdims=True)
        scaled = jnp.exp(shifted - peak)
        rounded = scaled.astype(BF16)
        m_ref[rows, :] = rounded
        peaks[rows, :] = jnp.broadcast_to(peak, (group, 128))
        totals[rows, :] = jnp.broadcast_to(jnp.sum(scaled, axis=1, keepdims=True), (group, 128))
        return carry

    lax.fori_loop(0, tile // group, some, 0, unroll=4)
    stat_ref[0:1, :] = jnp.transpose(peaks[...])[0:1, :]
    stat_ref[1:2, :] = jnp.transpose(totals[...])[0:1, :]
    stat_ref[2:3, :] = ids_ref[...]


def first_rows(logits, ids, stats, log_mass):
    rows, lists = logits.shape
    tile = min(512, rows)
    return pl.pallas_call(
        functools.partial(first_rows_kernel, parts=len(stats), log_mass=log_mass, group=32),
        grid=(rows // tile,),
        in_specs=[
            pl.BlockSpec((tile, lists), lambda i: (i, 0)),
            pl.BlockSpec((1, tile), lambda i: (0, i)),
        ]
        + [whole((2, lists))] * len(stats),
        out_specs=[
            pl.BlockSpec((tile, lists), lambda i: (i, 0)),
            pl.BlockSpec((3, tile), lambda i: (0, i)),
            whole((1, lists)),
        ],
        out_shape=[
            pltpu.VMEM((rows, lists), BF16),
            jax.ShapeDtypeStruct((3, rows), F32),
            jax.ShapeDtypeStruct((1, lists), F32),
        ],
        scratch_shapes=[pltpu.VMEM((tile, 128), F32), pltpu.VMEM((tile, 128), F32)],
        compiler_params=grant(24),
        cost_estimate=cost(4 * rows * lists, 6 * rows * lists, rows * lists),
        name="first_rows",
    )(in_vmem(logits), ids, *stats)


def store_parts(where, value):
    head = value.astype(BF16)
    rest = value - head.astype(F32)
    middle = rest.astype(BF16)
    last = (rest - middle.astype(F32)).astype(BF16)
    zero = jnp.zeros((5, value.shape[1]), BF16)
    where[...] = jnp.concatenate([head, middle, last, zero], axis=0)


def add_parts(sums):
    return (sums[2:3] + sums[1:2]) + sums[0:1]


def column_sum_kernel(*refs, parts, first):
    m_ref, own_ref = refs[0:2]
    stats = refs[2 : 2 + parts]
    weights = refs[-1]
    if first:
        out_ref, peak_ref = refs[2 + parts : 4 + parts]
    else:
        peak_ref, out_ref = refs[2 + parts : 4 + parts]

    @pl.when(pl.program_id(0) == 0)
    def _():
        if first:
            peak, total = join_pairs([part[...] for part in stats])
            peak_ref[...] = peak
        else:
            peak = peak_ref[...]
            total = tree([part[...] for part in stats], jnp.add)
        store_parts(weights, jnp.exp(own_ref[0:1, :] - (peak + jnp.log(total))))

    out_ref[...] = add_parts(
        lax.dot_general(weights[...], m_ref[...], NN, preferred_element_type=F32)
    )


def column_sums(scaled, own, stats, last, peak=None):
    rows, lists = scaled.shape
    tile = min(512, lists)
    first = peak is None
    row = whole((1, rows))
    kept = pl.BlockSpec(memory_space=pl.ANY)
    out_specs = [pl.BlockSpec((1, tile), lambda j: (0, j))]
    out_shape = [jax.ShapeDtypeStruct((1, lists), F32)]
    return pl.pallas_call(
        functools.partial(column_sum_kernel, parts=len(stats), first=first),
        grid=(lists // tile,),
        in_specs=[pl.BlockSpec((rows, tile), lambda j: (0, j)), whole(own.shape)]
        + [whole(stats[0].shape)] * len(stats)
        + ([] if first else [row]),
        out_specs=out_specs + ([row] if first else []) + ([] if last else [kept]),
        out_shape=out_shape
        + ([jax.ShapeDtypeStruct((1, rows), F32)] if first else [])
        + ([] if last else [pltpu.VMEM(scaled.shape, scaled.dtype)]),
        input_output_aliases={} if last else {0: 2 if first else 1},
        scratch_shapes=[pltpu.VMEM((8, rows), BF16)],
        compiler_params=grant(16),
        cost_estimate=cost(16 * rows * lists, 2 * rows * lists),
        name="column_sums",
    )(in_vmem(scaled), own, *stats, *([] if first else [peak]))


def row_sum_kernel(*refs, parts, ratio, log_mass):
    m_ref, first_ref, own_ref, peak_ref = refs[0:4]
    stats = refs[4 : 4 + parts]
    out_ref, col_ref, weights = refs[4 + parts], refs[5 + parts], refs[-1]

    @pl.when(pl.program_id(0) == 0)
    def _():
        total = tree([part[...] for part in stats], jnp.add)
        store_parts(weights, ratio / total)
        col_ref[...] = first_ref[...] + (log_mass - jnp.log(total))

    sums = add_parts(lax.dot_general(weights[...], m_ref[...], NT, preferred_element_type=F32))
    out_ref[...] = sums * jnp.exp(own_ref[0:1, :] - peak_ref[...])


def row_sums(scaled, first_column, own, peak, stats, ratio, last):
    rows, lists = scaled.shape
    tile = min(512, rows)
    column = whole((1, lists))
    return pl.pallas_call(
        functools.partial(
            row_sum_kernel, parts=len(stats), ratio=ratio, log_mass=math.log(ratio)
        ),
        grid=(rows // tile,),
        in_specs=[
            pl.BlockSpec((tile, lists), lambda i: (i, 0)),
            column,
            pl.BlockSpec((own.shape[0], tile), lambda i: (0, i)),
            pl.BlockSpec((1, tile), lambda i: (0, i)),
        ]
        + [column] * len(stats),
        out_specs=[
            pl.BlockSpec((1, tile), lambda i: (0, i)),
            column,
        ]
        + ([] if last else [pl.BlockSpec(memory_space=pl.ANY)]),
        out_shape=[
            jax.ShapeDtypeStruct((1, rows), F32),
            jax.ShapeDtypeStruct((1, lists), F32),
        ]
        + ([] if last else [pltpu.VMEM(scaled.shape, scaled.dtype)]),
        input_output_aliases={} if last else {0: 2},
        scratch_shapes=[pltpu.VMEM((8, lists), BF16)],
        compiler_params=grant(16),
        cost_estimate=cost(16 * rows * lists, 2 * rows * lists),
        name="row_sums",
    )(in_vmem(scaled), first_column, own, peak, *stats)


def block_sums(blocks):
    flat = [(index, item) for index, block in enumerate(blocks) for item in block]

    def logits(item):
        here = item[2]()
        return here, lax.dot_general(item[0], here, NT, preferred_element_type=F32)

    found = [None] * len(blocks)
    here, ready = logits(flat[0][1])
    for place, (index, item) in enumerate(flat):
        following = logits(flat[place + 1][1]) if place + 1 < len(flat) else (None, None)
        plan = jnp.exp(ready + item[3]() + item[1]).astype(BF16)
        part = lax.dot_general(plan, here, NN, preferred_element_type=F32)
        wide = plan.astype(F32)
        sums = wide[:, 0:128]
        for lane in range(128, wide.shape[1], 128):
            sums = sums + wide[:, lane : lane + 128]
        before = found[index]
        found[index] = (part, sums) if before is None else (before[0] + part, before[1] + sums)
        here, ready = following
    return found


def chunk(index, depth):
    return slice(index * depth, (index + 1) * depth)


def wide_column(col_ref):
    size = col_ref.shape[1]
    return jnp.transpose(jnp.broadcast_to(col_ref[...], (128, size)))[:, 0:1]


def loads(ref, rows, columns):
    return lambda: ref[rows, columns]


def own_plan_kernel(c_ref, col_ref, v_ref, r_ref, sum_ref, mass_ref, *, depth, part):
    doubled, column = c_ref[...] * 2, wide_column(col_ref)
    every = slice(None)
    parts = [slice(start, start + part) for start in range(0, doubled.shape[0], part)]
    blocks = [
        [
            (
                doubled[here],
                column[here],
                loads(v_ref, chunk(step, depth), every),
                loads(r_ref, every, chunk(step, depth)),
            )
            for step in range(v_ref.shape[0] // depth)
        ]
        for here in parts
    ]
    for here, (total, weight) in zip(parts, block_sums(blocks)):
        sum_ref[here, :] = total
        mass_ref[here, :] = weight


def own_plan(centroids, column, vectors, row):
    count, width = vectors.shape
    lists = centroids.shape[0]
    tile, depth = min(OWN_TILE, lists), min(1024, count)
    return pl.pallas_call(
        functools.partial(own_plan_kernel, depth=depth, part=min(256, lists)),
        grid=(lists // tile,),
        in_specs=[
            pl.BlockSpec((tile, width), lambda j: (j, 0)),
            pl.BlockSpec((1, tile), lambda j: (0, j)),
            whole((count, width)),
            whole((1, count)),
        ],
        out_specs=[
            pl.BlockSpec((tile, width), lambda j: (j, 0)),
            pl.BlockSpec((tile, 128), lambda j: (j, 0)),
        ],
        out_shape=[
            pltpu.HBM((lists, width), F32),
            pltpu.HBM((lists, 128), F32),
        ],
        compiler_params=grant(40),
        cost_estimate=cost(4 * count * lists * width, 4 * lists * width, count * lists),
        name="own_plan",
    )(in_hbm(centroids), column, in_hbm(vectors), row)


def plan_kernel(*refs, planes, owners, depth):
    others = planes - 1
    place_ref, c_ref, col_ref, sum_ref, mass_ref, ids_ref = refs[0:6]
    rows_in = refs[6 : 6 + others]
    halves = refs[6 + others : 6 + 3 * others]
    out_ref = refs[6 + 3 * others]
    picked = refs[7 + 3 * others : -3]
    held, chosen, sems = refs[-3:]
    tile = c_ref.shape[0]
    count = held.shape[0] // others
    piece = count // owners
    turn = pl.program_id(0)

    def copies(key):
        for index in range(owners):
            source = halves[2 * (key - 1) + index // (owners // 2)]
            at = (index % (owners // 2)) * piece
            slot = 2 * (index % (owners // 2)) + index // (owners // 2)
            start = (key - 1) * count + (place_ref[0] ^ slot) * piece
            yield pltpu.make_async_copy(
                source.at[pl.ds(at, piece)],
                held.at[pl.ds(pl.multiple_of(start, piece), piece)],
                sems.at[key - 1],
            )

    def wait(key):
        here = held.at[pl.ds((key - 1) * count, count)]
        pltpu.make_async_copy(here, here, sems.at[key - 1]).wait()

    def arriving(key):
        def load():
            wait(key)
            return held[chunk((key - 1) * (count // depth), depth), :]

        return load

    def compute(staged):
        doubled, column = c_ref[...] * 2, wide_column(col_ref)
        steps = count // depth
        every = slice(None)
        blocks = [
            [
                (
                    doubled,
                    column,
                    arriving(key)
                    if staged and step == 0
                    else loads(held, chunk((key - 1) * steps + step, depth), every),
                    loads(rows_in[key - 1], every, chunk(step, depth)),
                )
                for step in range(steps)
            ]
            for key in range(1, planes)
        ]
        found = [(sum_ref[...], mass_ref[...])] + block_sums(blocks)
        numerator = tree([item[0] for item in found], jnp.add)
        weight = tree([item[1] for item in found], jnp.add)
        fresh = (numerator / jnp.sum(weight, axis=1, keepdims=True)).astype(BF16)
        out_ref[...] = fresh
        slots = ids_ref.shape[0]
        lanes = lax.broadcasted_iota(jnp.int32, (slots, tile), 1) + turn * tile
        wanted = (ids_ref[...] == lanes).astype(F32).astype(BF16)
        return lax.dot_general(wanted, fresh, NN, preferred_element_type=F32)

    @pl.when(turn == 0)
    def _():
        for key in range(1, planes):
            for copy in copies(key):
                copy.start()
        chosen[...] = jnp.zeros_like(chosen)
        for key in range(1, planes):
            wait(key)

    chosen[...] += compute(False)

    @pl.when(turn == pl.num_programs(0) - 1)
    def _():
        each = ids_ref.shape[0] // len(picked)
        for index, piece_ref in enumerate(picked):
            piece_ref[...] = chosen[index * each : (index + 1) * each, :].astype(BF16)


def new_centroids(place, centroids, column, sums, masses, ids, rows, halves, owners):
    lists, width = centroids.shape
    others = len(rows)
    count = rows[0].shape[1]
    tile, depth = min(512, lists), min(1024, count)
    total = others * count
    return pl.pallas_call(
        functools.partial(plan_kernel, planes=others + 1, owners=owners, depth=depth),
        grid=(lists // tile,),
        in_specs=[
            pl.BlockSpec(memory_space=pltpu.SMEM),
            pl.BlockSpec((tile, width), lambda j: (j, 0)),
            pl.BlockSpec((1, tile), lambda j: (0, j)),
            pl.BlockSpec((tile, width), lambda j: (j, 0)),
            pl.BlockSpec((tile, 128), lambda j: (j, 0)),
            whole(ids.shape),
        ]
        + [whole((1, count))] * others
        + [pl.BlockSpec(memory_space=pl.ANY)] * len(halves),
        out_specs=[pl.BlockSpec((tile, width), lambda j: (j, 0))]
        + [whole((ids.shape[0] // owners, width))] * owners,
        out_shape=[jax.ShapeDtypeStruct((lists, width), BF16)]
        + [jax.ShapeDtypeStruct((ids.shape[0] // owners, width), BF16)] * owners,
        scratch_shapes=[
            pltpu.VMEM((total, width), BF16),
            pltpu.VMEM((ids.shape[0], width), F32),
            pltpu.SemaphoreType.DMA((others,)),
        ],
        compiler_params=grant(40),
        cost_estimate=cost(4 * total * lists * width, 2 * total * width, total * lists),
        name="new_centroids",
    )(
        place,
        in_hbm(centroids),
        column,
        in_hbm(sums),
        in_hbm(masses),
        ids,
        *rows,
        *halves,
    )


def residual_kernel(*refs):
    slot_ref, own_ref = refs[0:2]
    pieces = refs[2:-2]
    out_ref, table = refs[-2:]
    each = pieces[0].shape[0]
    for index, piece in enumerate(pieces):
        table[index * each : (index + 1) * each, :] = piece[...].astype(F32)
    count, slots = own_ref.shape[0], table.shape[0]
    wanted = slot_ref[...] == lax.broadcasted_iota(jnp.int32, (count, slots), 1)
    chosen = lax.dot_general(
        wanted.astype(F32).astype(BF16), table[...].astype(BF16), NN, preferred_element_type=F32
    )
    out_ref[...] = (own_ref[...].astype(F32) - chosen).astype(BF16)


def subtract_rows(slots, own, pieces):
    return pl.pallas_call(
        residual_kernel,
        out_shape=jax.ShapeDtypeStruct(own.shape, BF16),
        scratch_shapes=[pltpu.VMEM((len(pieces) * pieces[0].shape[0], own.shape[1]), F32)],
        compiler_params=grant(16),
        name="subtract_rows",
    )(slots, own, *pieces)


def join_kernel(*refs):
    pieces, out_ref, sems = refs[:-2], refs[-2], refs[-1]
    each = pieces[0].shape[0]
    moves = [
        pltpu.make_async_copy(piece, out_ref.at[pl.ds(index * each, each)], sems.at[index])
        for index, piece in enumerate(pieces)
    ]
    for move in moves:
        move.start()
    for move in moves:
        move.wait()


def join_pieces(pieces):
    each, width = pieces[0].shape
    anywhere = pl.BlockSpec(memory_space=pl.ANY)
    return pl.pallas_call(
        join_kernel,
        in_specs=[anywhere] * len(pieces),
        out_specs=anywhere,
        out_shape=pltpu.HBM((each * len(pieces), width), pieces[0].dtype),
        scratch_shapes=[pltpu.SemaphoreType.DMA((len(pieces),))],
        compiler_params=grant(4),
        cost_estimate=cost(0, 2 * each * len(pieces) * width),
        name="join_pieces",
    )(*[in_vmem(piece) for piece in pieces])


def swap(value, axis, key):
    count = lax.axis_size(axis)
    return lax.ppermute(value, axis, [(i, i ^ key) for i in range(count)])


def everywhere(value, axis, step=1):
    return [value] + [swap(value, axis, key) for key in range(step, lax.axis_size(axis), step)]


def after(value, *others):
    return lax.optimization_barrier((value,) + others)[0]


def step_on_device(vectors, centroids, assignment):
    row_count, _ = vectors.shape
    list_count = centroids.shape[0]
    data_count = lax.axis_size("dp")
    owner_count = lax.axis_size("cent")
    me = lax.axis_index("cent")
    place = me.astype(jnp.int32)[None]
    send_count = row_count // owner_count
    capacity = max(2, 2 * send_count // owner_count)
    slot_count = owner_count * capacity
    ratio = row_count * data_count / (list_count * owner_count)
    log_mass = math.log(ratio)

    own = lax.dynamic_slice_in_dim(vectors, me * send_count, send_count, 0)
    keys = jnp.bitwise_xor(assignment // list_count, me)
    local_ids = assignment % list_count
    positions = jnp.arange(send_count, dtype=jnp.int32)
    earlier_same = (keys[:, None] == keys[None, :]) & (positions[None, :] < positions[:, None])
    slots = keys * capacity + jnp.sum(earlier_same.astype(jnp.int32), axis=1)
    picked = slots[:, None] == jnp.arange(row_count, dtype=jnp.int32)[None, :]
    outgoing_ids = jnp.sum(jnp.where(picked, local_ids[:, None], 0), axis=0)
    ids_row = outgoing_ids.astype(F32)[None, :]

    def across(piece, *ready):
        return everywhere(after(piece, *ready), "cent", 2)

    def partners(pieces):
        half = join_pieces(pieces)
        return [half, swap(half, "cent", 1)]

    arriving = [swap(own, "dp", 1)]
    logits, stats = logits_and_stats(vectors, centroids)
    parts = everywhere(stats, "dp")
    if data_count > 2:
        arriving.append(swap(after(own, *parts), "dp", 2))
    moved = across(arriving[0], stats)
    scaled, own_stats, first_column = first_rows(logits, ids_row, parts, log_mass)
    partner = swap(own_stats, "cent", 1)
    pair = jnp.concatenate(
        join_pairs([own_stats, partner]) + (own_stats[2:3], partner[2:3]), axis=0
    )
    parts = everywhere(pair, "cent", 2)
    rows_of = [part[2 + key : 3 + key, :slot_count] for part in parts for key in range(2)]
    arrived = jnp.concatenate(
        [rows_of[key][0, key * capacity : (key + 1) * capacity] for key in range(owner_count)]
    ).astype(jnp.int32)

    peak = None
    halves = []
    for turn in range(1, ITERS):
        halves += partners(moved)
        moved = across(arriving[turn], pair)
        last = turn == ITERS - 1
        sums, *kept = column_sums(scaled, own_stats, parts, False, peak)
        peak = kept.pop(0) if turn == 1 else peak
        scaled = kept[0]
        parts = everywhere(sums, "dp")
        if turn == 1:
            for key in range(3, data_count):
                arriving.append(swap(after(own, *parts), "dp", key))
        sums, column, *kept = row_sums(scaled, first_column, own_stats, peak, parts, ratio, last)
        scaled = scaled if last else kept[0]
        partner = swap(sums, "cent", 1)
        pair = sums + partner
        parts = everywhere(pair, "cent", 2)
    halves += partners(moved)
    for turn in range(ITERS, data_count - 1):
        halves += partners(across(arriving[turn]))
    row = -(peak + jnp.log(tree(parts, jnp.add)))

    rows = everywhere(row, "dp")[1:]
    sums, masses = own_plan(centroids, column, vectors, row)
    updated, *pieces = new_centroids(
        place,
        centroids,
        column,
        sums,
        masses,
        arrived[:, None],
        rows,
        halves,
        owner_count,
    )
    pieces = [pieces[0]] + [swap(pieces[key], "cent", key) for key in range(1, owner_count)]
    residuals = subtract_rows(slots[:, None], own, pieces)
    return (updated, row.reshape(row_count), column.reshape(list_count), residuals)


def solution(mesh):
    in_specs = (P("dp", None), P("cent", None), P(("dp", "cent")))
    out_specs = (P("cent", None), P("dp"), P("cent"), P(("dp", "cent"), None))
    return jax.shard_map(
        step_on_device, mesh=mesh, in_specs=in_specs, out_specs=out_specs, check_vma=False
    )
```
